512 devices in a mesh: cols: 32 (over z, core), rep: 16 (over y, x).
Axes of the slice: x: 4, y: 4, z: 16, core: 2. Of those that a mesh axis runs over, the one named last changes fastest.
Arguments:
- hamiltonian_band: float32 [64, 5, 128, 128], P('cols'), may hold values from -0.25 to 0.25
- margin_factors: float32 [64, 256, 128], P('cols', 'rep'), may hold values from -0.25 to 0.25
- neighbour_mask: int32 [64, 5], P('cols'), may hold values from 0 to 1, as said below
- fermi_level: float32 [1], replicated, may hold values from -0.3 to 0.3
Outputs:
- density: float32 [64, 640, 640], P('cols', 'rep')
The draws below stay inside these ranges and needn't reach their ends.
Inputs may be any that keep to these rules, and one draw needn't show every extreme that they name: `neighbour_mask`: entry 2 of every row is 1; every row has 3 to 5 ones; some row has 5 ones and some row has exactly 3.
All inputs are finite; a program needn't handle non-finite values.
Results may differ from the reference program's by a relative error of at most 0.0003.
Values sent between devices are 32-bit elements; how exact they have to be, the bound alone decides.
A program may use at most 64 MiB of HBM per device.

```python
import jax
import jax.numpy as jnp
from jax import lax

B = 128
P_SIZE = 256
W = 2
ROOT = 2
SIGN = 2
NC = 5
M = 640
NB = 64


def draw_neighbour_mask(key, part):
    key_count, key_order = jax.random.split(jax.random.fold_in(key, 17))
    sides = 2 * W
    extra = jax.random.randint(key_count, (NB,), 2, sides + 1)
    extra = extra.at[0].set(sides).at[1].set(2)
    scores = jax.random.randint(key_order, (NB, sides), 0, 1 << 20) * sides + jnp.arange(sides, dtype=jnp.int32)[None, :]
    ranking = jnp.argsort(jnp.argsort(scores, axis=1, stable=True), axis=1, stable=True)
    chosen = (ranking < extra[:, None]).astype(jnp.int32)
    center = jnp.ones((NB, 1), jnp.int32)
    return jnp.concatenate([chosen[:, :W], center, chosen[:, W:]], axis=1)


def steps_of(key, shape, cuts, least, top_value):
    loudness = 1.0
    for axis_at, parts in cuts:
        draws = jax.random.uniform(jax.random.fold_in(jax.random.fold_in(key, 6), axis_at), (parts,), jnp.float32, least / len(cuts), top_value / len(cuts))
        loudness = loudness * jnp.repeat(jnp.exp(draws), shape[axis_at] // parts).reshape((-1,) + (1,) * (len(shape) - 1 - axis_at))
    return loudness


def centred(own_key, extent, scale, most, cuts=(), kind=jnp.bfloat16):
    array = jax.random.normal(own_key, extent, jnp.float32) * scale
    if len(cuts) > 0:
        array = steps_of(own_key, extent, cuts, -0.22, 0.18) * array
    return jnp.clip(array, min=-most, max=most).astype(kind)


def setup_inputs(seed: int = 0) -> dict:
    arg_keys = jax.random.split(jax.random.key(seed), 5)
    hamiltonian_band = centred(arg_keys[0], (NB, NC, B, B), M ** -0.5, 0.25, ((0, 32),), jnp.float32)
    margin_factors = centred(arg_keys[1], (NB, P_SIZE, B), M ** -0.5, 0.25, ((0, 32), (1, 16)), jnp.float32)
    neighbour_mask = draw_neighbour_mask(jax.random.fold_in(arg_keys[4], 71), 0)
    fermi_level = jnp.clip(jax.random.uniform(arg_keys[3], (1,), jnp.float32, -0.3, 0.3), -0.3, 0.3)
    return dict(hamiltonian_band=hamiltonian_band, margin_factors=margin_factors, neighbour_mask=neighbour_mask, fermi_level=fermi_level)


def matmul(left, right):
    return jnp.dot(left, right, preferred_element_type=jnp.float32, precision=lax.Precision.HIGHEST)

def mirror_blocks(band, mask_row):
    block_rows = []
    for left_idx in range(NC):
        block_line = []
        for right_idx in range(NC):
            if abs(left_idx - right_idx) <= W:
                pair = band[right_idx, left_idx - right_idx + W] + band[left_idx, W - left_idx + right_idx].T
                weight = mask_row[left_idx] * mask_row[right_idx]
                block_line.append(0.5 * pair * weight)
            else:
                block_line.append(jnp.zeros((B, B), jnp.float32))
        block_rows.append(jnp.concatenate(block_line, axis=1))
    return jnp.concatenate(block_rows, axis=0)

def reference(hamiltonian_band, margin_factors, neighbour_mask, fermi_level):
    identity = jnp.eye(M, dtype=jnp.float32)

    def one_column(column_id):
        offsets = jnp.arange(NC, dtype=jnp.int32) - W
        neighbours = ((column_id + offsets) % NB).astype(jnp.int32)
        mask_row = neighbour_mask[column_id].astype(jnp.float32)
        factors = margin_factors[neighbours] * mask_row[:, None, None]
        stacked = jnp.transpose(factors, (1, 0, 2)).reshape(P_SIZE, M)
        margin = identity + matmul(stacked.T, stacked)
        hamilton = mirror_blocks(hamiltonian_band[neighbours], mask_row)
        root_scale = 2.0 * jnp.sqrt(jnp.sum(margin * margin) / M)
        forward_iter = margin / root_scale
        inverse_iter = identity
        for iteration in range(ROOT):
            step_mat = 0.5 * (3.0 * identity - matmul(inverse_iter, forward_iter))
            forward_iter = matmul(forward_iter, step_mat)
            inverse_iter = matmul(inverse_iter, step_mat)
        inverse_iter = inverse_iter / jnp.sqrt(root_scale)
        ortho = matmul(inverse_iter, matmul(hamilton, inverse_iter))
        shifted = ortho - fermi_level[0] * identity
        spread = 2.0 * jnp.sqrt(jnp.sum(shifted * shifted) / M + 1e-05)
        sign_iter = shifted / spread
        for iteration in range(SIGN):
            square_mat = matmul(sign_iter, sign_iter)
            cube_mat = matmul(sign_iter, square_mat)
            sign_iter = 0.5 * (3.0 * sign_iter - cube_mat)
        return 0.5 * (identity - sign_iter)
    return lax.map(one_column, jnp.arange(NB, dtype=jnp.int32))
```

```python
import functools
import jax, jax.numpy as jnp
from jax import lax
from jax.experimental import pallas as pl
from jax.experimental.pallas import tpu as pltpu
B=128; NC=5; M=640; PS=256; ROWS=80
F32=jnp.float32; BF=jnp.bfloat16

def split(x):
    hi = x.astype(BF)
    return hi, (x - hi.astype(F32)).astype(BF)

def dot(a, b):
    return jnp.dot(a, b, preferred_element_type=F32)

def dot_nt(a, b):
    return lax.dot_general(a, b, (((1,), (1,)), ((), ())), preferred_element_type=F32)

def dot3(a, b, d=dot):
    (ah, al), (bh, bl) = a, b
    return d(ah, bh) + d(ah, bl) + d(al, bh)

def rows_kernel(mask_ref, fermi_ref, row_ref, y_ref, hb_ref, out_ref, h_ref, yt_ref, x_ref, lw_ref, rw_ref):
    for a in range(NC):
        blk = y_ref[a] * mask_ref[a]
        yt_ref[a*B:(a+1)*B, :] = blk.T
    yt = split(yt_ref[...])
    y_full = jnp.concatenate([y_ref[a] * mask_ref[a] for a in range(NC)], axis=1)
    y = split(y_full)
    for a in range(NC):
        for b in range(NC):
            sl = (slice(a*B, (a+1)*B), slice(b*B, (b+1)*B))
            if abs(a-b) <= 2:
                w = 0.5 * mask_ref[a] * mask_ref[b]
                h_ref[sl] = (hb_ref[b, a-b+2] + hb_ref[a, b-a+2].T) * w
            else:
                h_ref[sl] = jnp.zeros((B, B), F32)
    eye = (lax.broadcasted_iota(jnp.int32, (PS, PS), 0) == lax.broadcasted_iota(jnp.int32, (PS, PS), 1))
    k = dot3(y, yt)
    one = jnp.ones((1, 1), F32)
    sumsq = M * one + 2.0 * jnp.sum(jnp.where(eye, k, 0.0), keepdims=True) + jnp.sum(k*k, keepdims=True)
    c = 2.0 * jnp.sqrt(sumsq / M)
    al = 1.0 / c
    t = 0.5 * (3.0 - al)
    u = 0.5 * (3.0 - al * t * t)
    ks = split(k)
    k2 = dot3(ks, ks)
    b0 = al * t * (t - al); b1 = al * al * (0.25 * al - t); b2 = 0.25 * al * al * al
    bm = b1 * k + b2 * k2 + jnp.where(eye, b0, 0.0)
    kb = dot3(ks, split(bm))
    rs = lax.rsqrt(c)
    rm = (-0.5 * t * bm + 0.25 * al * kb - jnp.where(eye, 0.5 * al * u, 0.0)) * rs
    a0 = t * u * rs
    vt = dot3(yt, split(rm))
    vts = split(vt)
    pt = dot3(split(h_ref[...]), yt)
    n = dot3(y, split(pt))
    pt2 = a0 * pt + 0.5 * dot3(vts, split(n))
    w = dot3(split(pt2), vts, dot_nt)
    x_ref[...] = w
    mu = fermi_ref[0]
    a2 = a0 * a0
    acc = jnp.zeros((1, 1), F32)
    for a in range(NC):
        for b in range(NC):
            sl = (slice(a*B, (a+1)*B), slice(b*B, (b+1)*B))
            e = x_ref[sl] + x_ref[sl[1], sl[0]].T
            if abs(a-b) <= 2:
                e = e + a2 * h_ref[sl]
            if a == b:
                ey = (lax.broadcasted_iota(jnp.int32, (B, B), 0) == lax.broadcasted_iota(jnp.int32, (B, B), 1))
                e = e - jnp.where(ey, mu, 0.0)
            acc = acc + jnp.sum(e * e, keepdims=True)
            h_ref[sl] = e
    inv = 1.0 / (2.0 * jnp.sqrt(acc / M + 1e-5))
    x0 = h_ref[...] * inv
    xh, xl = split(x0)
    lw_ref[:, 0:M] = xh; lw_ref[:, M:2*M] = xl; lw_ref[:, 2*M:3*M] = xh
    rw_ref[0:M, :] = xh; rw_ref[M:2*M, :] = xh; rw_ref[2*M:3*M, :] = xl
    a_m = dot(lw_ref[...], rw_ref[...])
    ah, alo = split(a_m)
    rw_ref[0:M, :] = ah; rw_ref[M:2*M, :] = ah; rw_ref[2*M:3*M, :] = alo
    x1 = 1.5 * x0 - 0.5 * dot(lw_ref[...], rw_ref[...])
    x_ref[...] = x1
    xh, xl = split(x1)
    rw_ref[0:M, :] = xh; rw_ref[M:2*M, :] = xh; rw_ref[2*M:3*M, :] = xl
    r0 = pl.multiple_of(row_ref[0], 8)
    xr = x_ref[pl.ds(r0, ROWS), :]
    rh, rl = split(xr)
    q = dot(jnp.concatenate([rh, rl, rh], axis=1), rw_ref[...])
    qh, ql = split(q)
    cube = dot(jnp.concatenate([qh, ql, qh], axis=1), rw_ref[...])
    x2 = 1.5 * xr - 0.5 * cube
    ii = lax.broadcasted_iota(jnp.int32, (ROWS, M), 0) + r0
    jj = lax.broadcasted_iota(jnp.int32, (ROWS, M), 1)
    out_ref[...] = jnp.where(ii == jj, 0.5, 0.0) - 0.5 * x2

def rows_call(mask, fermi, row, y, hb):
    vm = pl.BlockSpec(memory_space=pltpu.VMEM); sm = pl.BlockSpec(memory_space=pltpu.SMEM)
    return pl.pallas_call(rows_kernel, out_shape=jax.ShapeDtypeStruct((ROWS, M), F32),
        in_specs=[sm, sm, sm, vm, vm], out_specs=vm,
        scratch_shapes=[pltpu.VMEM((M, M), F32), pltpu.VMEM((M, PS), F32), pltpu.VMEM((M, M), F32),
            pltpu.VMEM((M, 3*M), BF), pltpu.VMEM((3*M, M), BF)],
        compiler_params=pltpu.CompilerParams(vmem_limit_bytes=50<<20))(mask, fermi, row, y, hb)


from jax.sharding import PartitionSpec as P

def extended(block, axis="cols"):
    n = lax.axis_size(axis)
    fwd = [(i, (i + 1) % n) for i in range(n)]
    bwd = [(d, s) for s, d in fwd]
    low = lax.ppermute(block, axis, fwd)
    high = lax.ppermute(block, axis, bwd)
    return jnp.concatenate([low, block, high], axis=0)

def on_device(hamiltonian_band, margin_factors, neighbour_mask, fermi_level):
    rep = lax.axis_index("rep")
    g = rep % 2
    wide = extended(margin_factors)
    y = lax.all_gather(wide, "rep", axis=1, tiled=True)
    y = lax.dynamic_slice_in_dim(y, g, NC, 0)
    hb = lax.dynamic_slice_in_dim(extended(hamiltonian_band), g, NC, 0)
    mask = lax.dynamic_slice_in_dim(neighbour_mask, g, 1, 0)[0].astype(F32)
    row = (rep // 2) * ROWS
    rows = rows_call(mask, fermi_level, row[None].astype(jnp.int32), y, hb)
    first, second = rows[:40], rows[40:]
    keep = jnp.where(g == 0, first, second)
    send = jnp.where(g == 0, second, first)
    n = lax.axis_size("rep")
    got = lax.ppermute(send, "rep", [(i, i ^ 1) for i in range(n)])
    return jnp.stack([jnp.where(g == 0, keep, got), jnp.where(g == 0, got, keep)])

def solution(mesh):
    in_specs = (P("cols", None, None, None), P("cols", "rep", None), P("cols", None), P())
    return jax.shard_map(on_device, mesh=mesh, in_specs=in_specs, out_specs=P("cols", "rep", None), check_vma=False)
```

```python
import functools
import jax, jax.numpy as jnp
from jax import lax
from jax.experimental import pallas as pl
from jax.experimental.pallas import tpu as pltpu
from jax.sharding import PartitionSpec as P

B = 128
NC = 5
M = 640
PS = 256
ROWS = 80
PIECE = 40
SIDE = 4
F32 = jnp.float32
BF = jnp.bfloat16
MESH = pl.DeviceIdType.MESH


def split(x):
    hi = x.astype(BF)
    return hi, (x - hi.astype(F32)).astype(BF)


def dot(a, b):
    return jnp.dot(a, b, preferred_element_type=F32)


def dot_nt(a, b):
    return lax.dot_general(a, b, (((1,), (1,)), ((), ())), preferred_element_type=F32)


def dot3(a, b, d=dot):
    (ah, al), (bh, bl) = a, b
    return d(ah, bh) + d(ah, bl) + d(al, bh)


class Net:
    def __init__(self, send, recv):
        self.send, self.recv = send, recv
        self.slots = 0
        self.sent = []

    def slot(self):
        self.slots += 1
        return self.slots - 1

    def copy(self, slot, src, dst, dev):
        c = pltpu.make_async_remote_copy(
            src_ref=src, dst_ref=dst, send_sem=self.send.at[slot], recv_sem=self.recv.at[slot],
            device_id=dev, device_id_type=MESH)
        c.start()
        self.sent.append(c)

    def arrived(self, slot, dst, dev):
        pltpu.make_async_remote_copy(
            src_ref=dst, dst_ref=dst, send_sem=self.send.at[slot], recv_sem=self.recv.at[slot],
            device_id=dev, device_id_type=MESH).wait_recv()


SLOTS = 64


def gather(ncol, hb_ref, mf_ref, yb, hbuf, net, loc):
    c = lax.axis_index("cols")
    r = lax.axis_index("rep")
    y, x = r // SIDE, r % SIDE
    g = x % 2
    up, down = (c + 1) % ncol, (c + ncol - 1) % ncol
    xs = [x, (x + 3) % 4, (x + 1) % 4, (x + 2) % 4]
    ys = [y, (y + 3) % 4, (y + 1) % 4, (y + 2) % 4]
    dev_c = {+1: (up, r), -1: (down, r)}
    dev_x = {+1: (c, y * 4 + xs[2]), -1: (c, y * 4 + xs[1])}
    dev_y = {+1: (c, ys[2] * 4 + x), -1: (c, ys[1] * 4 + x)}
    barrier = pltpu.get_barrier_semaphore()
    for d in (dev_c, dev_x, dev_y):
        for s in (+1, -1):
            pl.semaphore_signal(barrier, inc=1, device_id=d[s], device_id_type=MESH)
    pl.semaphore_wait(barrier, 6)

    def at(h, w, p1, p2, n=None):
        ws = pl.ds(w, n) if n else slice(None)
        return yb.at[ws, h, p1, p2]

    first = {0: (xs, dev_x), 1: (ys, dev_y)}
    second = {0: (ys, dev_y), 1: (xs, dev_x)}
    cs = {(s, h): net.slot() for h in (0, 1) for s in (+1, -1)}
    for h in (0, 1):
        p1, p2 = second[h][0][0], first[h][0][0]
        for s, w in ((+1, 0), (-1, 4)):
            net.copy(cs[s, h], mf_ref.at[:, 8 * h:8 * h + 8], at(h, w, p1, p2, 2), dev_c[s])
    local = []
    for h in (0, 1):
        p1, p2 = second[h][0][0], first[h][0][0]
        l = pltpu.make_async_copy(mf_ref.at[:, 8 * h:8 * h + 8], at(h, 2, p1, p2, 2), loc.at[h])
        l.start()
        local.append(l)
    hs = [net.slot() for _ in range(3)]
    plans = {
        0: ([(+1, 1, 1, 1, 5), (+1, 0, 0, 2, 5), (-1, 0, 4, 0, 3)], [(0, 2, 0, 5), (1, 3, 0, 4)]),
        1: ([(-1, 0, 3, 0, 4), (-1, 1, 4, 0, 3), (+1, 1, 0, 2, 5)], [(1, 2, 0, 5), (0, 1, 1, 5)]),
    }
    for gg in (0, 1):
        @pl.when(g == gg)
        def _():
            for slot, (s, k, a, e0, e1) in zip(hs, plans[gg][0]):
                pltpu.make_async_remote_copy(
                    src_ref=hb_ref.at[k, e0:e1], dst_ref=hbuf.at[a, e0:e1], send_sem=net.send.at[slot],
                    recv_sem=net.recv.at[slot], device_id=dev_c[s], device_id_type=MESH).start()
            for i, (k, a, e0, e1) in enumerate(plans[gg][1]):
                pltpu.make_async_copy(hb_ref.at[k, e0:e1], hbuf.at[a, e0:e1], loc.at[2 + i]).start()

    s1 = {(h, s): net.slot() for h in (0, 1) for s in (+1, -1)}
    s1r = {(h, s): net.slot() for h in (0, 1) for s in (+1, -1)}
    s2 = {(h, p, s): net.slot() for h in (0, 1) for p in range(4) for s in (+1, -1)}
    s2r = {(h, p, s): net.slot() for h in (0, 1) for p in range(4) for s in (+1, -1)}

    def span2(h):
        return (g, 5) if h == 0 else (0, 6)

    def parts2(h):
        return ((g, 3), (g + 3, 2)) if h == 0 else ((0, 3), (3, 3))

    def send2(h, p):
        qs, dev = second[h]
        pos = first[h][0][p]
        w, n = span2(h)
        for s in (+1, -1):
            ref = at(h, w, qs[0], pos, n)
            net.copy(s2[h, p, s], ref, ref, dev[s])

    def relay2(h, p):
        qs, dev = second[h]
        pos = first[h][0][p]
        w, n = span2(h)
        for s, q, (w0, n0) in ((+1, qs[1], parts2(h)[0]), (-1, qs[2], parts2(h)[1])):
            net.arrived(s2[h, p, s], at(h, w, q, pos, n), dev[-s])
            ref = at(h, w0, q, pos, n0)
            net.copy(s2r[h, p, s], ref, ref, dev[s])

    for h in (0, 1):
        qs, ps = second[h][0], first[h][0]
        local[h].wait()
        for s, w in ((+1, 0), (-1, 4)):
            net.arrived(cs[s, h], at(h, w, qs[0], ps[0], 2), dev_c[-s])
        for s in (+1, -1):
            ref = at(h, 0, qs[0], ps[0], 6)
            net.copy(s1[h, s], ref, ref, first[h][1][s])
    for h in (0, 1):
        send2(h, 0)
    for h in (0, 1):
        qs, (ps, dev) = second[h][0], first[h]
        for s, p, w in ((+1, 1, 0), (-1, 2, 3)):
            net.arrived(s1[h, s], at(h, 0, qs[0], ps[p], 6), dev[-s])
            ref = at(h, w, qs[0], ps[p], 3)
            net.copy(s1r[h, s], ref, ref, dev[s])
    for h in (0, 1):
        send2(h, 1)
        send2(h, 2)
    for h in (0, 1):
        relay2(h, 0)
    for h in (0, 1):
        qs, (ps, dev) = second[h][0], first[h]
        for s, w in ((+1, 0), (-1, 3)):
            net.arrived(s1r[h, s], at(h, w, qs[0], ps[3], 3), dev[-s])
        send2(h, 3)
    for p in (1, 2, 3):
        for h in (0, 1):
            relay2(h, p)
    for gg in (0, 1):
        @pl.when(g == gg)
        def _():
            for slot, (s, k, a, e0, e1) in zip(hs, plans[gg][0]):
                d = pltpu.make_async_remote_copy(
                    src_ref=hb_ref.at[k, e0:e1], dst_ref=hbuf.at[a, e0:e1], send_sem=net.send.at[slot],
                    recv_sem=net.recv.at[slot], device_id=dev_c[s], device_id_type=MESH)
                d.wait()
            for i, (k, a, e0, e1) in enumerate(plans[gg][1]):
                pltpu.make_async_copy(hb_ref.at[k, e0:e1], hbuf.at[a, e0:e1], loc.at[2 + i]).wait()
    for p in range(4):
        for h in (0, 1):
            qs, dev = second[h]
            for s, (w0, n0) in ((+1, parts2(h)[0]), (-1, parts2(h)[1])):
                net.arrived(s2r[h, p, s], at(h, w0, qs[3], first[h][0][p], n0), dev[-s])


def fused(ncol, mask_ref, fermi_ref, hb_ref, mf_ref, out_ref, yb, hbuf, h_ref, yt_ref, x_ref, lw_ref, rw_ref,
          stage, send, recv, loc):
    c = lax.axis_index("cols")
    r = lax.axis_index("rep")
    g = r % 2
    net = Net(send, recv)
    gather(ncol, hb_ref, mf_ref, yb, hbuf, net, loc)
    mask = [mask_ref[g, a].astype(F32) for a in range(NC)]
    ys = [yb[g + a].reshape(PS, B) * mask[a] for a in range(NC)]
    for a in range(NC):
        yt_ref[a * B:(a + 1) * B, :] = ys[a].T
    yt = split(yt_ref[...])
    y = split(jnp.concatenate(ys, axis=1))
    for a in range(NC):
        for b in range(NC):
            sl = (slice(a * B, (a + 1) * B), slice(b * B, (b + 1) * B))
            if abs(a - b) <= 2:
                w = 0.5 * mask[a] * mask[b]
                h_ref[sl] = (hbuf[b, a - b + 2] + hbuf[a, b - a + 2].T) * w
            else:
                h_ref[sl] = jnp.zeros((B, B), F32)
    eye = lax.broadcasted_iota(jnp.int32, (PS, PS), 0) == lax.broadcasted_iota(jnp.int32, (PS, PS), 1)
    k = dot3(y, yt)
    one = jnp.ones((1, 1), F32)
    sumsq = M * one + 2.0 * jnp.sum(jnp.where(eye, k, 0.0), keepdims=True) + jnp.sum(k * k, keepdims=True)
    cs = 2.0 * jnp.sqrt(sumsq / M)
    al = 1.0 / cs
    t = 0.5 * (3.0 - al)
    u = 0.5 * (3.0 - al * t * t)
    ks = split(k)
    k2 = dot3(ks, ks)
    b0 = al * t * (t - al)
    b1 = al * al * (0.25 * al - t)
    b2 = 0.25 * al * al * al
    bm = b1 * k + b2 * k2 + jnp.where(eye, b0, 0.0)
    kb = dot3(ks, split(bm))
    rs = lax.rsqrt(cs)
    rm = (-0.5 * t * bm + 0.25 * al * kb - jnp.where(eye, 0.5 * al * u, 0.0)) * rs
    a0 = t * u * rs
    vts = split(dot3(yt, split(rm)))
    pt = dot3(split(h_ref[...]), yt)
    n = dot3(y, split(pt))
    pt2 = a0 * pt + 0.5 * dot3(vts, split(n))
    x_ref[...] = dot3(split(pt2), vts, dot_nt)
    mu = fermi_ref[0]
    a2 = a0 * a0
    acc = jnp.zeros((1, 1), F32)
    for a in range(NC):
        for b in range(NC):
            sl = (slice(a * B, (a + 1) * B), slice(b * B, (b + 1) * B))
            e = x_ref[sl] + x_ref[sl[1], sl[0]].T
            if abs(a - b) <= 2:
                e = e + a2 * h_ref[sl]
            if a == b:
                ey = lax.broadcasted_iota(jnp.int32, (B, B), 0) == lax.broadcasted_iota(jnp.int32, (B, B), 1)
                e = e - jnp.where(ey, mu, 0.0)
            acc = acc + jnp.sum(e * e, keepdims=True)
            h_ref[sl] = e
    inv = 1.0 / (2.0 * jnp.sqrt(acc / M + 1e-5))
    x0 = h_ref[...] * inv
    xh, xl = split(x0)
    lw_ref[:, 0:M] = xh
    lw_ref[:, M:2 * M] = xl
    lw_ref[:, 2 * M:3 * M] = xh
    rw_ref[0:M, :] = xh
    rw_ref[M:2 * M, :] = xh
    rw_ref[2 * M:3 * M, :] = xl
    ah, alo = split(dot(lw_ref[...], rw_ref[...]))
    rw_ref[0:M, :] = ah
    rw_ref[M:2 * M, :] = ah
    rw_ref[2 * M:3 * M, :] = alo
    x1 = 1.5 * x0 - 0.5 * dot(lw_ref[...], rw_ref[...])
    x_ref[...] = x1
    xh, xl = split(x1)
    rw_ref[0:M, :] = xh
    rw_ref[M:2 * M, :] = xh
    rw_ref[2 * M:3 * M, :] = xl
    r0 = pl.multiple_of((r // 2) * ROWS, 8)
    xr = x_ref[pl.ds(r0, ROWS), :]
    rh, rl = split(xr)
    q = dot(jnp.concatenate([rh, rl, rh], axis=1), rw_ref[...])
    qh, ql = split(q)
    cube = dot(jnp.concatenate([qh, ql, qh], axis=1), rw_ref[...])
    x2 = 1.5 * xr - 0.5 * cube
    ii = lax.broadcasted_iota(jnp.int32, (ROWS, M), 0) + r0
    jj = lax.broadcasted_iota(jnp.int32, (ROWS, M), 1)
    stage[...] = jnp.where(ii == jj, 0.5, 0.0) - 0.5 * x2
    partner = (c, r + 1 - 2 * g)
    fs = net.slot()
    theirs = stage.at[pl.ds(pl.multiple_of(PIECE * (1 - g), 8), PIECE)]
    net.copy(fs, theirs, out_ref.at[g], partner)
    out_ref[g] = stage[pl.ds(pl.multiple_of(PIECE * g, 8), PIECE)]
    for s in net.sent:
        s.wait_send()
    net.arrived(fs, out_ref.at[1 - g], partner)
    assert net.slots <= SLOTS


def on_device(ncol, hamiltonian_band, margin_factors, neighbour_mask, fermi_level):
    vm = pl.BlockSpec(memory_space=pltpu.VMEM)
    sm = pl.BlockSpec(memory_space=pltpu.SMEM)
    return pl.pallas_call(
        functools.partial(fused, ncol),
        out_shape=jax.ShapeDtypeStruct((2, PIECE, M), F32),
        in_specs=[sm, sm, pl.BlockSpec(memory_space=pl.ANY), vm],
        out_specs=vm,
        scratch_shapes=[
            pltpu.VMEM((6, 2, 4, 4, 8, B), F32),
            pltpu.VMEM((NC, NC, B, B), F32),
            pltpu.VMEM((M, M), F32),
            pltpu.VMEM((M, PS), F32),
            pltpu.VMEM((M, M), F32),
            pltpu.VMEM((M, 3 * M), BF),
            pltpu.VMEM((3 * M, M), BF),
            pltpu.VMEM((ROWS, M), F32),
            pltpu.SemaphoreType.DMA((SLOTS,)),
            pltpu.SemaphoreType.DMA((SLOTS,)),
            pltpu.SemaphoreType.DMA((4,)),
        ],
        compiler_params=pltpu.CompilerParams(collective_id=0, has_side_effects=True, vmem_limit_bytes=50 << 20),
    )(neighbour_mask, fermi_level, hamiltonian_band, margin_factors)


def solution(mesh):
    in_specs = (P("cols", None, None, None), P("cols", "rep", None), P("cols", None), P())
    return jax.shard_map(
        functools.partial(on_device, mesh.shape["cols"]), mesh=mesh, in_specs=in_specs,
        out_specs=P("cols", "rep", None), check_vma=False)
```

```python
import functools
import jax, jax.numpy as jnp
from jax import lax
from jax.experimental import pallas as pl
from jax.experimental.pallas import tpu as pltpu
from jax.sharding import PartitionSpec as P

B = 128
NC = 5
M = 640
PS = 256
ROWS = 80
PIECE = 40
SIDE = 4
F32 = jnp.float32
BF = jnp.bfloat16
MESH = pl.DeviceIdType.MESH


def split(x):
    hi = x.astype(BF)
    return hi, (x - hi.astype(F32)).astype(BF)


def dot(a, b):
    return jnp.dot(a, b, preferred_element_type=F32)


def dot_nt(a, b):
    return lax.dot_general(a, b, (((1,), (1,)), ((), ())), preferred_element_type=F32)


def dot3(a, b, d=dot):
    (ah, al), (bh, bl) = a, b
    return d(ah, bh) + d(ah, bl) + d(al, bh)


class Net:
    def __init__(self, send, recv):
        self.send, self.recv = send, recv
        self.slots = 0
        self.sent = []

    def slot(self):
        self.slots += 1
        return self.slots - 1

    def copy(self, slot, src, dst, dev):
        c = pltpu.make_async_remote_copy(
            src_ref=src, dst_ref=dst, send_sem=self.send.at[slot], recv_sem=self.recv.at[slot],
            device_id=dev, device_id_type=MESH)
        c.start()
        self.sent.append(c)

    def arrived(self, slot, dst, dev):
        pltpu.make_async_remote_copy(
            src_ref=dst, dst_ref=dst, send_sem=self.send.at[slot], recv_sem=self.recv.at[slot],
            device_id=dev, device_id_type=MESH).wait_recv()


SLOTS = 96
TILES = ((0, 256), (256, 512), (512, 640))
BLOCKS = {
    0: {+1: ((1, 1, 1, 5), (0, 0, 2, 5)), -1: ((0, 4, 0, 3),)},
    1: {+1: ((1, 0, 2, 5),), -1: ((0, 3, 0, 4), (1, 4, 0, 3))},
}
OWN = {0: ((0, 2, 0, 5), (1, 3, 0, 4)), 1: ((1, 2, 0, 5), (0, 1, 1, 5))}
OFFSETS = (0, 1, 3, 2)


def gather(ncol, c, r, g, gd, hb_ref, mf_ref, yb, hbuf, net, loc):
    y, x = r // SIDE, r % SIDE
    up, down = (c + 1) % ncol, (c + ncol - 1) % ncol
    cols = {0: c, +1: up, -1: down}

    def dev(dc, h, dp):
        if h == 0:
            return (cols[dc], y * SIDE + (x + dp) % SIDE)
        return (cols[dc], ((y + dp) % SIDE) * SIDE + x)

    barrier = pltpu.get_barrier_semaphore()
    partners = [dev(dc, h, dp) for h in (0, 1) for dp in OFFSETS for dc in (0, +1, -1)
                if not (dp == 0 and (dc == 0 or h == 1))]
    for d in partners:
        pl.semaphore_signal(barrier, inc=1, device_id=d, device_id_type=MESH)
    pl.semaphore_wait(barrier, len(partners))

    mine = {0: x, 1: y}

    def at(h, w, n, second, first):
        return yb.at[pl.ds(w, n), h, second, first]

    group = {0: 2, +1: 0, -1: 4}
    s1 = {(h, dc, dp): net.slot() for h in (0, 1) for dc in (0, +1, -1) for dp in OFFSETS if (dc, dp) != (0, 0)}
    order = ([(h, dc, 0) for h in (0, 1) for dc in (+1, -1)]
             + [(h, dc, dp) for dp in (2, 1, 3) for h in (0, 1) for dc in (+1, -1, 0)])
    for h, dc, dp in order:
        net.copy(s1[h, dc, dp], mf_ref.at[:, 8 * h:8 * h + 8], at(h, group[dc], 2, mine[1 - h], mine[h]), dev(dc, h, dp))
    local = []
    for h in (0, 1):
        l = pltpu.make_async_copy(mf_ref.at[:, 8 * h:8 * h + 8], at(h, 2, 2, mine[1 - h], mine[h]), loc.at[h])
        l.start()
        local.append(l)
    hs = {(s, i): net.slot() for s in (+1, -1) for i in (0, 1)}

    def blocks(s, i, k, a, e0, e1):
        return pltpu.make_async_remote_copy(
            src_ref=hb_ref.at[k, e0:e1], dst_ref=hbuf.at[a, e0:e1], send_sem=net.send.at[hs[s, i]],
            recv_sem=net.recv.at[hs[s, i]], device_id=dev(s, 0, 0), device_id_type=MESH)

    for gg in (0, 1):
        @pl.when(gd == gg)
        def _():
            for s in (+1, -1):
                for i, b in enumerate(BLOCKS[gg][s]):
                    blocks(s, i, *b).start()

        @pl.when(g == gg)
        def _():
            for i, (k, a, e0, e1) in enumerate(OWN[gg]):
                pltpu.make_async_copy(hb_ref.at[k, e0:e1], hbuf.at[a, e0:e1], loc.at[2 + i]).start()

    s2 = {(h, dp, s): net.slot() for h in (0, 1) for dp in OFFSETS for s in (+1, -1)}
    s2r = {(h, dp, s): net.slot() for h in (0, 1) for dp in OFFSETS for s in (+1, -1)}
    halves = {+1: (0, 3), -1: (3, 3)}

    def place(h, dp):
        return (mine[h] + 4 - dp) % SIDE

    def along(h, s):
        return dev(0, 1 - h, s)

    def second(h, s):
        return (mine[1 - h] + 4 + s) % SIDE

    for dp in OFFSETS:
        for h in (0, 1):
            if dp == 0:
                local[h].wait()
            for dc in (0, +1, -1):
                if (dc, dp) != (0, 0):
                    net.arrived(s1[h, dc, dp], at(h, group[dc], 2, mine[1 - h], place(h, dp)), dev(0, h, dp))
            ref = at(h, 0, 6, mine[1 - h], place(h, dp))
            for s in (+1, -1):
                net.copy(s2[h, dp, s], ref, ref, along(h, s))
    for dp in OFFSETS:
        for h in (0, 1):
            for s in (+1, -1):
                net.arrived(s2[h, dp, s], at(h, 0, 6, second(h, -s), place(h, dp)), along(h, -s))
                ref = at(h, *halves[s], second(h, -s), place(h, dp))
                net.copy(s2r[h, dp, s], ref, ref, along(h, s))
    for gg in (0, 1):
        @pl.when(g == gg)
        def _():
            for s in (+1, -1):
                for i, b in enumerate(BLOCKS[gg][s]):
                    blocks(s, i, *b).wait_recv()
            for i, (k, a, e0, e1) in enumerate(OWN[gg]):
                pltpu.make_async_copy(hb_ref.at[k, e0:e1], hbuf.at[a, e0:e1], loc.at[2 + i]).wait()
    for dp in OFFSETS:
        for h in (0, 1):
            for s in (+1, -1):
                net.arrived(s2r[h, dp, s], at(h, *halves[s], second(h, 2), place(h, dp)), along(h, -s))

    def finish():
        for gg in (0, 1):
            @pl.when(gd == gg)
            def _():
                for s in (+1, -1):
                    for i, b in enumerate(BLOCKS[gg][s]):
                        blocks(s, i, *b).wait_send()
    return finish


def cat3l(a, b):
    return jnp.concatenate([a, b, a], axis=1)


def cdot(a, b):
    return dot(cat3l(*a), jnp.concatenate([b[0], b[0], b[1]], axis=0))


def fused(ncol, mask_hbm, fermi_hbm, hb_ref, mf_ref, out_ref, yb, hbuf, h_ref, yt_ref, x_ref, eh_ref, el_ref,
          stage, mask_ref, fermi_ref, send, recv, loc):
    c = lax.axis_index("cols")
    r = lax.axis_index("rep")
    y, x = r // SIDE, r % SIDE
    core = c % 2
    g = (x * (1 - core) + y * core) % 2
    gd = (x * core + y * (1 - core)) % 2
    other = r + (1 - 2 * g) * (1 + 3 * core)
    small = [pltpu.make_async_copy(mask_hbm, mask_ref, loc.at[4]), pltpu.make_async_copy(fermi_hbm, fermi_ref, loc.at[5])]
    for s in small:
        s.start()
    net = Net(send, recv)
    finish = gather(ncol, c, r, g, gd, hb_ref, mf_ref, yb, hbuf, net, loc)
    for s in small:
        s.wait()
    mask = [mask_ref[g, a].astype(F32) for a in range(NC)]
    mu = fermi_ref[0]
    ys = [yb[g + a].reshape(PS, B) * mask[a] for a in range(NC)]
    for a in range(NC):
        yt_ref[a * B:(a + 1) * B, :] = ys[a].T
    yt = split(yt_ref[...])
    yy = split(jnp.concatenate(ys, axis=1))
    for a in range(NC):
        for b in range(NC):
            sl = (slice(a * B, (a + 1) * B), slice(b * B, (b + 1) * B))
            if abs(a - b) <= 2:
                w = 0.5 * mask[a] * mask[b]
                h_ref[sl] = (hbuf[b, a - b + 2] + hbuf[a, b - a + 2].T) * w
            else:
                h_ref[sl] = jnp.zeros((B, B), F32)
    eye = lax.broadcasted_iota(jnp.int32, (PS, PS), 0) == lax.broadcasted_iota(jnp.int32, (PS, PS), 1)
    k = cdot(yy, yt)
    ks = split(k)
    k2 = cdot(ks, ks)
    k3 = cdot(ks, split(k2))
    pt = cdot(split(h_ref[...]), yt)
    n = cdot(yy, split(pt))
    one = jnp.ones((1, 1), F32)
    sumsq = M * one + 2.0 * jnp.sum(jnp.where(eye, k, 0.0), keepdims=True) + jnp.sum(k * k, keepdims=True)
    cs = 2.0 * jnp.sqrt(sumsq / M)
    al = 1.0 / cs
    t = 0.5 * (3.0 - al)
    u = 0.5 * (3.0 - al * t * t)
    b0 = al * t * (t - al)
    b1 = al * al * (0.25 * al - t)
    b2 = 0.25 * al * al * al
    rs = lax.rsqrt(cs)
    q0 = (-0.5 * t * b0 - 0.5 * al * u) * rs
    q1 = (-0.5 * t * b1 + 0.25 * al * b0) * rs
    q2 = (-0.5 * t * b2 + 0.25 * al * b1) * rs
    q3 = (0.25 * al * b2) * rs
    a0 = t * u * rs
    rm = q1 * k + q2 * k2 + q3 * k3 + jnp.where(eye, q0, 0.0)
    vts = split(cdot(yt, split(rm)))
    pts = split(a0 * pt + 0.5 * cdot(vts, split(n)))
    a2 = a0 * a0
    lh, ll = (jnp.concatenate([pts[i], vts[i]], axis=1) for i in (0, 1))
    rh, rl = (jnp.concatenate([vts[i], pts[i]], axis=1) for i in (0, 1))
    lcat = cat3l(lh, ll)
    rcat = jnp.concatenate([rh, rh, rl], axis=1)
    acc = jnp.zeros((1, 1), F32)
    for c0, c1 in TILES:
        e = dot_nt(lcat, rcat[c0:c1]) + a2 * h_ref[:, c0:c1]
        ii = lax.broadcasted_iota(jnp.int32, e.shape, 0)
        jj = lax.broadcasted_iota(jnp.int32, e.shape, 1) + c0
        e = e - jnp.where(ii == jj, mu, 0.0)
        acc = acc + jnp.sum(e * e, keepdims=True)
        eh_ref[:, c0:c1], el_ref[:, c0:c1] = split(e)
        x_ref[:, c0:c1] = e
    inv = 1.0 / (2.0 * jnp.sqrt(acc / M + 1e-5))

    def times(v, c0=0, c1=M):
        hi, lo = split(v)
        p = dot(jnp.concatenate([hi, lo], axis=0), eh_ref[:, c0:c1])
        return (p[:ROWS] + p[ROWS:] + dot(hi, el_ref[:, c0:c1])) * inv

    mine = pl.multiple_of(r * PIECE, 8)
    theirs = pl.multiple_of(other * PIECE, 8)
    x0 = jnp.concatenate([x_ref[pl.ds(mine, PIECE)], x_ref[pl.ds(theirs, PIECE)]], axis=0) * inv
    x1 = 1.5 * x0 - 0.5 * times(times(x0))
    p = times(x1)
    q = 1.5 * p - 0.5 * times(times(p))
    p = times(q)
    p2 = times(p)
    partner = (c, other)
    fs = [net.slot() for _ in TILES]
    for slot, (c0, c1) in zip(fs, TILES):
        x2 = 1.5 * x1[:, c0:c1] - 0.5 * (1.5 * p[:, c0:c1] - 0.5 * times(p2, c0, c1))
        ii = lax.broadcasted_iota(jnp.int32, (PIECE, c1 - c0), 0)
        jj = lax.broadcasted_iota(jnp.int32, (PIECE, c1 - c0), 1) + c0
        stage[:, c0:c1] = jnp.where(ii + theirs == jj, 0.5, 0.0) - 0.5 * x2[PIECE:]
        net.copy(slot, stage.at[:, c0:c1], out_ref.at[g, :, c0:c1], partner)
        out_ref[g, :, c0:c1] = jnp.where(ii + mine == jj, 0.5, 0.0) - 0.5 * x2[:PIECE]
    for s in net.sent:
        s.wait_send()
    finish()
    for slot, (c0, c1) in zip(fs, TILES):
        net.arrived(slot, out_ref.at[1 - g, :, c0:c1], partner)
    assert net.slots <= SLOTS


def on_device(ncol, hamiltonian_band, margin_factors, neighbour_mask, fermi_level):
    vm = pl.BlockSpec(memory_space=pltpu.VMEM)
    return pl.pallas_call(
        functools.partial(fused, ncol),
        out_shape=jax.ShapeDtypeStruct((2, PIECE, M), F32),
        in_specs=[pl.BlockSpec(memory_space=pltpu.HBM)] * 4,
        out_specs=vm,
        scratch_shapes=[
            pltpu.VMEM((6, 2, 4, 4, 8, B), F32),
            pltpu.VMEM((NC, NC, B, B), F32),
            pltpu.VMEM((M, M), F32),
            pltpu.VMEM((M, PS), F32),
            pltpu.VMEM((M, M), F32),
            pltpu.VMEM((M, M), BF),
            pltpu.VMEM((M, M), BF),
            pltpu.VMEM((PIECE, M), F32),
            pltpu.SMEM((2, NC), jnp.int32),
            pltpu.SMEM((1,), F32),
            pltpu.SemaphoreType.DMA((SLOTS,)),
            pltpu.SemaphoreType.DMA((SLOTS,)),
            pltpu.SemaphoreType.DMA((6,)),
        ],
        compiler_params=pltpu.CompilerParams(collective_id=0, has_side_effects=True, vmem_limit_bytes=63 << 20),
    )(neighbour_mask, fermi_level, hamiltonian_band, margin_factors)


def solution(mesh):
    in_specs = (P("cols", None, None, None), P("cols", "rep", None), P("cols", None), P())
    return jax.shard_map(
        functools.partial(on_device, mesh.shape["cols"]), mesh=mesh, in_specs=in_specs,
        out_specs=P("cols", "rep", None), check_vma=False)
```

```python
import functools
import jax, jax.numpy as jnp
from jax import lax
from jax.experimental import pallas as pl
from jax.experimental.pallas import tpu as pltpu
from jax.sharding import PartitionSpec as P

B = 128
NC = 5
M = 640
PS = 256
ROWS = 80
PIECE = 40
SIDE = 4
F32 = jnp.float32
BF = jnp.bfloat16
MESH = pl.DeviceIdType.MESH


def split(x):
    hi = x.astype(BF)
    return hi, (x - hi.astype(F32)).astype(BF)


def dot(a, b):
    return jnp.dot(a, b, preferred_element_type=F32)


def dot_nt(a, b):
    return lax.dot_general(a, b, (((1,), (1,)), ((), ())), preferred_element_type=F32)


def dot3(a, b, d=dot):
    (ah, al), (bh, bl) = a, b
    return d(ah, bh) + d(ah, bl) + d(al, bh)


class Net:
    def __init__(self, send, recv):
        self.send, self.recv = send, recv
        self.slots = 0
        self.sent = []

    def slot(self):
        self.slots += 1
        return self.slots - 1

    def copy(self, slot, src, dst, dev):
        c = pltpu.make_async_remote_copy(
            src_ref=src, dst_ref=dst, send_sem=self.send.at[slot], recv_sem=self.recv.at[slot],
            device_id=dev, device_id_type=MESH)
        c.start()
        self.sent.append(c)

    def arrived(self, slot, dst, dev):
        pltpu.make_async_remote_copy(
            src_ref=dst, dst_ref=dst, send_sem=self.send.at[slot], recv_sem=self.recv.at[slot],
            device_id=dev, device_id_type=MESH).wait_recv()


SLOTS = 64
TILES = ((0, 256), (256, 512), (512, 640))
BLOCKS = {
    0: {+1: ((1, 1, 1, 5), (0, 0, 2, 5)), -1: ((0, 4, 0, 3),)},
    1: {+1: ((1, 0, 2, 5),), -1: ((0, 3, 0, 4), (1, 4, 0, 3))},
}
OWN = {0: ((0, 2, 0, 5), (1, 3, 0, 4)), 1: ((1, 2, 0, 5), (0, 1, 1, 5))}
OFFSETS = (0, 1, 3, 2)


def gather(ncol, c, r, g, gd, hb_ref, mf_ref, yb, hbuf, net, loc, far_sem, between):
    y, x = lax.div(r, SIDE), lax.rem(r, SIDE)
    core = lax.rem(c, 2)
    mate = c + 1 - 2 * core
    far = lax.rem(c + ncol - 1 + 2 * core, ncol)

    def dev(col, h, dp):
        if h == 0:
            return (col, y * SIDE + (lax.rem(x + dp + 4, SIDE) if dp else x))
        return (col, (lax.rem(y + dp + 4, SIDE) if dp else y) * SIDE + x)

    def cross(col):
        return [dev(col, h, dp) for h in (0, 1) for dp in OFFSETS if not (dp == 0 and h == 1)]

    def greet(sem, d):
        pl.semaphore_signal(sem, inc=1, device_id=d, device_id_type=MESH)

    barrier = pltpu.get_barrier_semaphore()
    near = cross(c)[1:] + cross(mate)
    for d in near:
        greet(barrier, d)

    @pl.when(core == 0)
    def _():
        for d in cross(far):
            greet(barrier, d)
    pl.semaphore_wait(barrier, len(near) + 7 * core)

    mine = {0: x, 1: y}

    def at(h, w, n, second, first):
        return yb.at[pl.ds(w, n), h, second, first]

    def own(h):
        return mf_ref.at[:, 8 * h:8 * h + 8]

    w_mate, w_far = 4 * (1 - core), 4 * core
    sl_own = {(h, dp): net.slot() for h in (0, 1) for dp in OFFSETS[1:]}
    sl_mate = {(h, dp): net.slot() for h in (0, 1) for dp in OFFSETS}
    sl_far = {(h, dp): net.slot() for h in (0, 1) for dp in OFFSETS}
    hs = {(s, i): net.slot() for s in (+1, -1) for i in (0, 1)}

    def far_copy(h, dp):
        return pltpu.make_async_remote_copy(
            src_ref=own(h), dst_ref=at(h, 4 * (1 - core), 2, mine[1 - h], mine[h]),
            send_sem=net.send.at[sl_far[h, dp]], recv_sem=net.recv.at[sl_far[h, dp]],
            device_id=dev(far, h, dp), device_id_type=MESH)

    def blocks(s, i, k, a, e0, e1):
        to = lax.rem(c + ncol + s, ncol)
        return pltpu.make_async_remote_copy(
            src_ref=hb_ref.at[k, e0:e1], dst_ref=hbuf.at[a, e0:e1], send_sem=net.send.at[hs[s, i]],
            recv_sem=net.recv.at[hs[s, i]], device_id=(to, r), device_id_type=MESH)

    def far_sends(on):
        for dp in (2, 1, 3, 0):
            for h in (0, 1):
                far_copy(h, dp).start()
        for gg in (0, 1):
            @pl.when(gd == gg)
            def _():
                s = 2 * on - 1
                for i, b in enumerate(BLOCKS[gg][s]):
                    blocks(s, i, *b).start()

    @pl.when(core == 1)
    def _():
        for d in cross(far):
            greet(far_sem, d)
        far_sends(1)
    for dp in (2, 1, 3, 0):
        for h in (0, 1):
            net.copy(sl_mate[h, dp], own(h), at(h, 4 * core, 2, mine[1 - h], mine[h]), dev(mate, h, dp))
            if dp:
                net.copy(sl_own[h, dp], own(h), at(h, 2, 2, mine[1 - h], mine[h]), dev(c, h, dp))
    local = []
    for h in (0, 1):
        l = pltpu.make_async_copy(own(h), at(h, 2, 2, mine[1 - h], mine[h]), loc.at[h])
        l.start()
        local.append(l)
    for gg in (0, 1):
        for on in (0, 1):
            @pl.when((core == on) & (gd == gg))
            def _():
                s = 1 - 2 * on
                for i, b in enumerate(BLOCKS[gg][s]):
                    blocks(s, i, *b).start()

        @pl.when(g == gg)
        def _():
            for i, (k, a, e0, e1) in enumerate(OWN[gg]):
                pltpu.make_async_copy(hb_ref.at[k, e0:e1], hbuf.at[a, e0:e1], loc.at[2 + i]).start()

    start = {0: 2 - 2 * core, 1: w_far}
    half = {0: 2, 1: 1}
    keys = [(u, h, s) for u in (0, 1) for h in (0, 1) for s in (+1, -1)]
    s2 = {key + (p,): net.slot() for key in keys for p in (0, 1)}
    s2r = {key: net.slot() for key in keys}
    lead = {+1: 0, -1: 1}

    def place(h, dp):
        return lax.rem(mine[h] + 4 - dp, SIDE)

    def along(h, s):
        return dev(c, 1 - h, s)

    def second(h, s):
        return lax.rem(mine[1 - h] + 4 + s, SIDE)

    def rows(u, h, p, q):
        return yb.at[pl.ds(start[u] + p * half[u], half[u]), h, q]

    def send2(u, h):
        for first in (True, False):
            for s in (+1, -1):
                p = lead[s] if first else 1 - lead[s]
                ref = rows(u, h, p, mine[1 - h])
                net.copy(s2[u, h, s, p], ref, ref, along(h, s))

    def relay2(u, h):
        for s in (+1, -1):
            ref = rows(u, h, lead[s], second(h, -s))
            net.arrived(s2[u, h, s, lead[s]], ref, along(h, -s))
            net.copy(s2r[u, h, s], ref, ref, along(h, s))

    def last2(u, h):
        for s in (+1, -1):
            p = 1 - lead[s]
            net.arrived(s2[u, h, s, p], rows(u, h, p, second(h, -s)), along(h, -s))
            net.arrived(s2r[u, h, s], rows(u, h, lead[s], second(h, 2)), along(h, -s))

    def answer(when):
        @pl.when(when)
        def _():
            pl.semaphore_wait(far_sem, 7)
            far_sends(0)

    for h in (0, 1):
        local[h].wait()
        for dp in OFFSETS:
            if dp:
                net.arrived(sl_own[h, dp], at(h, 2, 2, mine[1 - h], place(h, dp)), along(h, 1))
            net.arrived(sl_mate[h, dp], at(h, w_mate, 2, mine[1 - h], place(h, dp)), along(h, 1))
        send2(0, h)
    answer((core == 0) & (c > 0))
    for h in (0, 1):
        relay2(0, h)
    for h in (0, 1):
        for dp in OFFSETS:
            net.arrived(sl_far[h, dp], at(h, w_far, 2, mine[1 - h], place(h, dp)), along(h, 1))
        send2(1, h)
    for h in (0, 1):
        relay2(1, h)
    for h in (0, 1):
        last2(0, h)
    answer(c == 0)
    for gg in (0, 1):
        @pl.when(g == gg)
        def _():
            for s in (+1, -1):
                for i, b in enumerate(BLOCKS[gg][s]):
                    blocks(s, i, *b).wait_recv()
            for i, (k, a, e0, e1) in enumerate(OWN[gg]):
                pltpu.make_async_copy(hb_ref.at[k, e0:e1], hbuf.at[a, e0:e1], loc.at[2 + i]).wait()
    between()
    for h in (0, 1):
        last2(1, h)

    def finish():
        for h in (0, 1):
            for dp in OFFSETS:
                far_copy(h, dp).wait_send()
        for gg in (0, 1):
            @pl.when(gd == gg)
            def _():
                for s in (+1, -1):
                    for i, b in enumerate(BLOCKS[gg][s]):
                        blocks(s, i, *b).wait_send()
    return finish


def cat3l(a, b):
    return jnp.concatenate([a, b, a], axis=1)


def cdot(a, b):
    return dot(cat3l(*a), jnp.concatenate([b[0], b[0], b[1]], axis=0))


def fused(ncol, mask_hbm, fermi_hbm, hb_ref, mf_ref, out_ref, yb, hbuf, h_ref, yt_ref, x_ref, eh_ref, el_ref,
          stage, mask_ref, fermi_ref, send, recv, loc, far_sem):
    c = lax.axis_index("cols")
    r = lax.axis_index("rep")
    y, x = lax.div(r, SIDE), lax.rem(r, SIDE)
    core = lax.rem(c, 2)
    g = lax.rem(x * (1 - core) + y * core, 2)
    gd = lax.rem(x * core + y * (1 - core), 2)
    other = r + (1 - 2 * g) * (1 + 3 * core)
    small = [pltpu.make_async_copy(mask_hbm, mask_ref, loc.at[4]), pltpu.make_async_copy(fermi_hbm, fermi_ref, loc.at[5])]
    for s in small:
        s.start()
    net = Net(send, recv)
    mask = []

    def between():
        for o in small:
            o.wait()
        mask.extend(mask_ref[g, a].astype(F32) for a in range(NC))
        for a in range(NC):
            for b in range(NC):
                sl = (slice(a * B, (a + 1) * B), slice(b * B, (b + 1) * B))
                if abs(a - b) <= 2:
                    w = 0.5 * mask[a] * mask[b]
                    h_ref[sl] = (hbuf[b, a - b + 2] + hbuf[a, b - a + 2].T) * w
                else:
                    h_ref[sl] = jnp.zeros((B, B), F32)

    finish = gather(ncol, c, r, g, gd, hb_ref, mf_ref, yb, hbuf, net, loc, far_sem, between)
    mu = fermi_ref[0]
    ys = [yb[g + a].reshape(PS, B) * mask[a] for a in range(NC)]
    for a in range(NC):
        yt_ref[a * B:(a + 1) * B, :] = ys[a].T
    yt = split(yt_ref[...])
    yy = split(jnp.concatenate(ys, axis=1))
    eye = lax.broadcasted_iota(jnp.int32, (PS, PS), 0) == lax.broadcasted_iota(jnp.int32, (PS, PS), 1)
    k = cdot(yy, yt)
    ks = split(k)
    k2 = cdot(ks, ks)
    k3 = cdot(ks, split(k2))
    pt = cdot(split(h_ref[...]), yt)
    n = cdot(yy, split(pt))
    one = jnp.ones((1, 1), F32)
    sumsq = M * one + 2.0 * jnp.sum(jnp.where(eye, k, 0.0), keepdims=True) + jnp.sum(k * k, keepdims=True)
    cs = 2.0 * jnp.sqrt(sumsq / M)
    al = 1.0 / cs
    t = 0.5 * (3.0 - al)
    u = 0.5 * (3.0 - al * t * t)
    b0 = al * t * (t - al)
    b1 = al * al * (0.25 * al - t)
    b2 = 0.25 * al * al * al
    rs = lax.rsqrt(cs)
    q0 = (-0.5 * t * b0 - 0.5 * al * u) * rs
    q1 = (-0.5 * t * b1 + 0.25 * al * b0) * rs
    q2 = (-0.5 * t * b2 + 0.25 * al * b1) * rs
    q3 = (0.25 * al * b2) * rs
    a0 = t * u * rs
    rm = q1 * k + q2 * k2 + q3 * k3 + jnp.where(eye, q0, 0.0)
    vts = split(cdot(yt, split(rm)))
    pts = split(a0 * pt + 0.5 * cdot(vts, split(n)))
    a2 = a0 * a0
    lh, ll = (jnp.concatenate([pts[i], vts[i]], axis=1) for i in (0, 1))
    rh, rl = (jnp.concatenate([vts[i], pts[i]], axis=1) for i in (0, 1))
    lcat = cat3l(lh, ll)
    rcat = jnp.concatenate([rh, rh, rl], axis=1)
    acc = jnp.zeros((1, 1), F32)
    for c0, c1 in TILES:
        e = dot_nt(lcat, rcat[c0:c1]) + a2 * h_ref[:, c0:c1]
        ii = lax.broadcasted_iota(jnp.int32, e.shape, 0)
        jj = lax.broadcasted_iota(jnp.int32, e.shape, 1) + c0
        e = e - jnp.where(ii == jj, mu, 0.0)
        acc = acc + jnp.sum(e * e, keepdims=True)
        eh_ref[:, c0:c1], el_ref[:, c0:c1] = split(e)
        x_ref[:, c0:c1] = e
    inv = 1.0 / (2.0 * jnp.sqrt(acc / M + 1e-5))

    def times(v, c0=0, c1=M):
        hi, lo = split(v)
        p = dot(jnp.concatenate([hi, lo], axis=0), eh_ref[:, c0:c1])
        return (p[:ROWS] + p[ROWS:] + dot(hi, el_ref[:, c0:c1])) * inv

    mine = pl.multiple_of(r * PIECE, 8)
    theirs = pl.multiple_of(other * PIECE, 8)
    x0 = jnp.concatenate([x_ref[pl.ds(mine, PIECE)], x_ref[pl.ds(theirs, PIECE)]], axis=0) * inv
    x1 = 1.5 * x0 - 0.5 * times(times(x0))
    p = times(x1)
    q = 1.5 * p - 0.5 * times(times(p))
    p = times(q)
    p2 = times(p)
    partner = (c, other)
    fs = [net.slot() for _ in TILES]
    for slot, (c0, c1) in zip(fs, TILES):
        x2 = 1.5 * x1[:, c0:c1] - 0.5 * (1.5 * p[:, c0:c1] - 0.5 * times(p2, c0, c1))
        ii = lax.broadcasted_iota(jnp.int32, (PIECE, c1 - c0), 0)
        jj = lax.broadcasted_iota(jnp.int32, (PIECE, c1 - c0), 1) + c0
        stage[:, c0:c1] = jnp.where(ii + theirs == jj, 0.5, 0.0) - 0.5 * x2[PIECE:]
        net.copy(slot, stage.at[:, c0:c1], out_ref.at[g, :, c0:c1], partner)
        out_ref[g, :, c0:c1] = jnp.where(ii + mine == jj, 0.5, 0.0) - 0.5 * x2[:PIECE]
    for s in net.sent:
        s.wait_send()
    finish()
    for slot, (c0, c1) in zip(fs, TILES):
        net.arrived(slot, out_ref.at[1 - g, :, c0:c1], partner)
    assert net.slots <= SLOTS


def on_device(ncol, hamiltonian_band, margin_factors, neighbour_mask, fermi_level):
    vm = pl.BlockSpec(memory_space=pltpu.VMEM)
    return pl.pallas_call(
        functools.partial(fused, ncol),
        out_shape=jax.ShapeDtypeStruct((2, PIECE, M), F32),
        in_specs=[pl.BlockSpec(memory_space=pltpu.HBM)] * 4,
        out_specs=vm,
        scratch_shapes=[
            pltpu.VMEM((6, 2, 4, 4, 8, B), F32),
            pltpu.VMEM((NC, NC, B, B), F32),
            pltpu.VMEM((M, M), F32),
            pltpu.VMEM((M, PS), F32),
            pltpu.VMEM((M, M), F32),
            pltpu.VMEM((M, M), BF),
            pltpu.VMEM((M, M), BF),
            pltpu.VMEM((PIECE, M), F32),
            pltpu.SMEM((2, NC), jnp.int32),
            pltpu.SMEM((1,), F32),
            pltpu.SemaphoreType.DMA((SLOTS,)),
            pltpu.SemaphoreType.DMA((SLOTS,)),
            pltpu.SemaphoreType.DMA((6,)),
            pltpu.SemaphoreType.REGULAR,
        ],
        compiler_params=pltpu.CompilerParams(collective_id=0, has_side_effects=True, vmem_limit_bytes=(107 << 19)),
    )(neighbour_mask, fermi_level, hamiltonian_band, margin_factors)


def solution(mesh):
    in_specs = (P("cols", None, None, None), P("cols", "rep", None), P("cols", None), P())
    return jax.shard_map(
        functools.partial(on_device, mesh.shape["cols"]), mesh=mesh, in_specs=in_specs,
        out_specs=P("cols", "rep", None), check_vma=False)
```

```python
import functools
import jax, jax.numpy as jnp
from jax import lax
from jax.experimental import pallas as pl
from jax.experimental.pallas import tpu as pltpu
from jax.sharding import PartitionSpec as P

B = 128
NC = 5
M = 640
PS = 256
ROWS = 80
PIECE = 40
SIDE = 4
F32 = jnp.float32
BF = jnp.bfloat16
MESH = pl.DeviceIdType.MESH


def split(x):
    hi = x.astype(BF)
    return hi, (x - hi.astype(F32)).astype(BF)


def dot(a, b):
    return jnp.dot(a, b, preferred_element_type=F32)


def dot_nt(a, b):
    return lax.dot_general(a, b, (((1,), (1,)), ((), ())), preferred_element_type=F32)


def dot3(a, b, d=dot):
    (ah, al), (bh, bl) = a, b
    return d(ah, bh) + d(ah, bl) + d(al, bh)


class Net:
    def __init__(self, send, recv):
        self.send, self.recv = send, recv
        self.slots = 0
        self.sent = []

    def slot(self):
        self.slots += 1
        return self.slots - 1

    def copy(self, slot, src, dst, dev):
        c = pltpu.make_async_remote_copy(
            src_ref=src, dst_ref=dst, send_sem=self.send.at[slot], recv_sem=self.recv.at[slot],
            device_id=dev, device_id_type=MESH)
        c.start()
        self.sent.append(c)

    def arrived(self, slot, dst, dev):
        pltpu.make_async_remote_copy(
            src_ref=dst, dst_ref=dst, send_sem=self.send.at[slot], recv_sem=self.recv.at[slot],
            device_id=dev, device_id_type=MESH).wait_recv()


SLOTS = 64
TILES = ((0, 256), (256, 512), (512, 640))
BLOCKS = {
    0: {+1: ((1, 1, 1, 5), (0, 0, 2, 3), (0, 0, 3, 5)), -1: ((0, 4, 0, 3),)},
    1: {+1: ((1, 0, 2, 5),), -1: ((0, 3, 0, 4), (1, 4, 0, 3))},
}
OWN = {0: ((0, 2, 0, 5), (1, 3, 0, 4)), 1: ((1, 2, 0, 5), (0, 1, 1, 5))}
OFFSETS = (0, 1, 3, 2)


def gather(ncol, c, r, g, gd, hb_ref, mf_ref, yb, hbuf, net, loc, near_sem, far_sem, yfar, between):
    y, x = lax.div(r, SIDE), lax.rem(r, SIDE)
    core = lax.rem(c, 2)
    mate = c + 1 - 2 * core
    far = lax.rem(c + ncol - 1 + 2 * core, ncol)

    def dev(col, h, dp):
        if h == 0:
            return (col, y * SIDE + (lax.rem(x + dp + 4, SIDE) if dp else x))
        return (col, (lax.rem(y + dp + 4, SIDE) if dp else y) * SIDE + x)

    def cross(col):
        return [dev(col, h, dp) for h in (0, 1) for dp in OFFSETS if not (dp == 0 and h == 1)]

    def greet(sem, d):
        pl.semaphore_signal(sem, inc=1, device_id=d, device_id_type=MESH)

    barrier = pltpu.get_barrier_semaphore()
    home = c - core

    @pl.when(core == 0)
    def _():
        for d in cross(c)[1:]:
            greet(barrier, d)
        for q in range(SIDE * SIDE):
            greet(barrier, (far, q))

    @pl.when(core == 1)
    def _():
        for d in cross(home):
            greet(barrier, d)
    pl.semaphore_wait(barrier, 13 + 3 * core)

    mine = {0: x, 1: y}

    def at(h, w, n, second, first):
        return yb.at[pl.ds(w, n), h, second, first]

    def own(h):
        return mf_ref.at[:, 8 * h:8 * h + 8]

    w_mate, w_far = 4 * (1 - core), 4 * core
    sl_own = {(h, dp): net.slot() for h in (0, 1) for dp in OFFSETS[1:]}
    sl_mate = {(h, dp): net.slot() for h in (0, 1) for dp in OFFSETS}
    sl_far = [net.slot() for _ in range(SIDE * SIDE)]
    got_far = sl_far[0]
    hs = {(s, i): net.slot() for s in (+1, -1) for i in (0, 1, 2)}

    def needed(to_core, gg):
        return ((0, 2) if gg == 0 else (1, 2)) if to_core == 0 else ((0, 1) if gg == 0 else (0, 2))

    def far_copy(on, q):
        k0, k1 = needed(1 - on, q % 2 if on else q // SIDE % 2)
        return pltpu.make_async_remote_copy(
            src_ref=mf_ref.at[k0:k1], dst_ref=yfar.at[k0:k1, y, x],
            send_sem=net.send.at[sl_far[q]], recv_sem=net.recv.at[got_far],
            device_id=(far, q), device_id_type=MESH)

    def blocks(s, i, k, a, e0, e1, shift=0):
        to = lax.rem(c + ncol + s, ncol)
        return pltpu.make_async_remote_copy(
            src_ref=hb_ref.at[k, e0:e1], dst_ref=hbuf.at[a, e0:e1], send_sem=net.send.at[hs[s, i]],
            recv_sem=net.recv.at[hs[s, i]], device_id=(to, r - shift), device_id_type=MESH)

    def far_blocks(on, op):
        for gg in (0, 1):
            @pl.when(gd == gg)
            def _():
                s = 2 * on - 1
                for i, b in enumerate(BLOCKS[gg][s]):
                    if (s, i) != (+1, 2):
                        op(blocks(s, i, *b))
                if (on, gg) == (1, 1):
                    op(blocks(+1, 2, *BLOCKS[0][+1][2], shift=1))

    def far_sends(on):
        for q in range(SIDE * SIDE):
            far_copy(on, q).start()
        far_blocks(on, lambda d: d.start())

    @pl.when(core == 0)
    def _():
        greet(near_sem, (mate, r))

    @pl.when(core == 1)
    def _():
        for q in range(SIDE * SIDE):
            greet(far_sem, (far, q))
        far_sends(1)
        pl.semaphore_wait(near_sem, 1)
    for dp in (2, 1, 3, 0):
        for h in (0, 1):
            net.copy(sl_mate[h, dp], own(h), at(h, 4 * core, 2, mine[1 - h], mine[h]), dev(mate, h, dp))
            if dp:
                net.copy(sl_own[h, dp], own(h), at(h, 2, 2, mine[1 - h], mine[h]), dev(c, h, dp))
    local = []
    for h in (0, 1):
        l = pltpu.make_async_copy(own(h), at(h, 2, 2, mine[1 - h], mine[h]), loc.at[h])
        l.start()
        local.append(l)
    for gg in (0, 1):
        for on in (0, 1):
            @pl.when((core == on) & (gd == gg))
            def _():
                s = 1 - 2 * on
                for i, b in enumerate(BLOCKS[gg][s]):
                    blocks(s, i, *b).start()

        @pl.when(g == gg)
        def _():
            for i, (k, a, e0, e1) in enumerate(OWN[gg]):
                pltpu.make_async_copy(hb_ref.at[k, e0:e1], hbuf.at[a, e0:e1], loc.at[2 + i]).start()

    start = {0: 2 - 2 * core, 1: w_far}
    half = {0: 2, 1: 1}
    keys = [(u, h, s) for u in (0,) for h in (0, 1) for s in (+1, -1)]
    s2 = {key + (p,): net.slot() for key in keys for p in (0, 1)}
    s2r = {key: net.slot() for key in keys}
    lead = {+1: 0, -1: 1}

    def place(h, dp):
        return lax.rem(mine[h] + 4 - dp, SIDE)

    def along(h, s):
        return dev(c, 1 - h, s)

    def second(h, s):
        return lax.rem(mine[1 - h] + 4 + s, SIDE)

    def rows(u, h, p, q):
        return yb.at[pl.ds(start[u] + p * half[u], half[u]), h, q]

    def send2(u, h):
        for first in (True, False):
            for s in (+1, -1):
                p = lead[s] if first else 1 - lead[s]
                ref = rows(u, h, p, mine[1 - h])
                net.copy(s2[u, h, s, p], ref, ref, along(h, s))

    def relay2(u, h):
        for s in (+1, -1):
            ref = rows(u, h, lead[s], second(h, -s))
            net.arrived(s2[u, h, s, lead[s]], ref, along(h, -s))
            net.copy(s2r[u, h, s], ref, ref, along(h, s))

    def last2(u, h):
        for s in (+1, -1):
            p = 1 - lead[s]
            net.arrived(s2[u, h, s, p], rows(u, h, p, second(h, -s)), along(h, -s))
            net.arrived(s2r[u, h, s], rows(u, h, lead[s], second(h, 2)), along(h, -s))

    def answer(when):
        @pl.when(when)
        def _():
            pl.semaphore_wait(far_sem, SIDE * SIDE)
            far_sends(0)

    for h in (0, 1):
        local[h].wait()
        for dp in OFFSETS:
            if dp:
                net.arrived(sl_own[h, dp], at(h, 2, 2, mine[1 - h], place(h, dp)), along(h, 1))
            net.arrived(sl_mate[h, dp], at(h, w_mate, 2, mine[1 - h], place(h, dp)), along(h, 1))
        send2(0, h)
    answer((core == 0) & (c > 0))
    for h in (0, 1):
        relay2(0, h)
    for h in (0, 1):
        last2(0, h)
    answer(c == 0)

    def far_rows():
        for gg in (0, 1):
            for on in (0, 1):
                @pl.when((core == on) & (g == gg))
                def _():
                    k0, k1 = needed(on, gg)
                    net.arrived(got_far, yfar.at[k0:k1], (far, r))
        for k in (0, 1):
            yb[w_far + k, 0] = yfar[k, :, :, 0:8]
            for p in range(SIDE):
                for q in range(SIDE):
                    yb[w_far + k, 1, p, q] = yfar[k, q, p, 8:16]

    def far_band():
        for gg in (0, 1):
            @pl.when(g == gg)
            def _():
                for s in (+1, -1):
                    for i, b in enumerate(BLOCKS[gg][s]):
                        blocks(s, i, *b).wait_recv()
                for i, (k, a, e0, e1) in enumerate(OWN[gg]):
                    pltpu.make_async_copy(hb_ref.at[k, e0:e1], hbuf.at[a, e0:e1], loc.at[2 + i]).wait()
        between()

    def finish():
        for on in (0, 1):
            @pl.when(core == on)
            def _():
                for q in range(SIDE * SIDE):
                    far_copy(on, q).wait_send()
                far_blocks(on, lambda d: d.wait_send())
                for gg in (0, 1):
                    @pl.when(gd == gg)
                    def _():
                        s = 1 - 2 * on
                        for i, b in enumerate(BLOCKS[gg][s]):
                            blocks(s, i, *b).wait_send()
    return far_rows, far_band, finish


def cat3l(a, b):
    return jnp.concatenate([a, b, a], axis=1)


def cdot(a, b):
    return dot(cat3l(*a), jnp.concatenate([b[0], b[0], b[1]], axis=0))


def fused(ncol, mask_hbm, fermi_hbm, hb_ref, mf_ref, out_ref, yb, hbuf, h_ref, yt_ref, x_ref, eh_ref, el_ref,
          stage, yfar, mask_ref, fermi_ref, send, recv, loc, near_sem, far_sem):
    c = lax.axis_index("cols")
    r = lax.axis_index("rep")
    y, x = lax.div(r, SIDE), lax.rem(r, SIDE)
    core = lax.rem(c, 2)
    g = lax.rem(x * (1 - core) + y * core, 2)
    gd = lax.rem(x * core + y * (1 - core), 2)
    other = r + (1 - 2 * g) * (1 + 3 * core)
    small = [pltpu.make_async_copy(mask_hbm, mask_ref, loc.at[4]), pltpu.make_async_copy(fermi_hbm, fermi_ref, loc.at[5])]
    for s in small:
        s.start()
    net = Net(send, recv)
    mask = []

    def between():
        for a in range(NC):
            for b in range(NC):
                sl = (slice(a * B, (a + 1) * B), slice(b * B, (b + 1) * B))
                if abs(a - b) <= 2:
                    w = 0.5 * mask[a] * mask[b]
                    h_ref[sl] = (hbuf[b, a - b + 2] + hbuf[a, b - a + 2].T) * w
                else:
                    h_ref[sl] = jnp.zeros((B, B), F32)

    far_rows, far_band, finish = gather(
        ncol, c, r, g, gd, hb_ref, mf_ref, yb, hbuf, net, loc, near_sem, far_sem, yfar, between)
    for o in small:
        o.wait()
    mask.extend(mask_ref[g, a].astype(F32) for a in range(NC))
    far_rows()
    mu = fermi_ref[0]
    ys = [yb[g + a].reshape(PS, B) * mask[a] for a in range(NC)]
    for a in range(NC):
        yt_ref[a * B:(a + 1) * B, :] = ys[a].T
    yt = split(yt_ref[...])
    yy = split(jnp.concatenate(ys, axis=1))
    eye = lax.broadcasted_iota(jnp.int32, (PS, PS), 0) == lax.broadcasted_iota(jnp.int32, (PS, PS), 1)
    k = cdot(yy, yt)
    ks = split(k)
    k2 = cdot(ks, ks)
    k3 = cdot(ks, split(k2))
    far_band()
    pt = cdot(split(h_ref[...]), yt)
    n = cdot(yy, split(pt))
    one = jnp.ones((1, 1), F32)
    sumsq = M * one + 2.0 * jnp.sum(jnp.where(eye, k, 0.0), keepdims=True) + jnp.sum(k * k, keepdims=True)
    cs = 2.0 * jnp.sqrt(sumsq / M)
    al = 1.0 / cs
    t = 0.5 * (3.0 - al)
    u = 0.5 * (3.0 - al * t * t)
    b0 = al * t * (t - al)
    b1 = al * al * (0.25 * al - t)
    b2 = 0.25 * al * al * al
    rs = lax.rsqrt(cs)
    q0 = (-0.5 * t * b0 - 0.5 * al * u) * rs
    q1 = (-0.5 * t * b1 + 0.25 * al * b0) * rs
    q2 = (-0.5 * t * b2 + 0.25 * al * b1) * rs
    q3 = (0.25 * al * b2) * rs
    a0 = t * u * rs
    rm = q1 * k + q2 * k2 + q3 * k3 + jnp.where(eye, q0, 0.0)
    vts = split(cdot(yt, split(rm)))
    pts = split(a0 * pt + 0.5 * cdot(vts, split(n)))
    a2 = a0 * a0
    lh, ll = (jnp.concatenate([pts[i], vts[i]], axis=1) for i in (0, 1))
    rh, rl = (jnp.concatenate([vts[i], pts[i]], axis=1) for i in (0, 1))
    lcat = cat3l(lh, ll)
    rcat = jnp.concatenate([rh, rh, rl], axis=1)
    acc = jnp.zeros((1, 1), F32)
    for c0, c1 in TILES:
        e = dot_nt(lcat, rcat[c0:c1]) + a2 * h_ref[:, c0:c1]
        ii = lax.broadcasted_iota(jnp.int32, e.shape, 0)
        jj = lax.broadcasted_iota(jnp.int32, e.shape, 1) + c0
        e = e - jnp.where(ii == jj, mu, 0.0)
        acc = acc + jnp.sum(e * e, keepdims=True)
        eh_ref[:, c0:c1], el_ref[:, c0:c1] = split(e)
        x_ref[:, c0:c1] = e
    inv = 1.0 / (2.0 * jnp.sqrt(acc / M + 1e-5))

    def times(v, c0=0, c1=M):
        hi, lo = split(v)
        p = dot(jnp.concatenate([hi, lo], axis=0), eh_ref[:, c0:c1])
        return (p[:ROWS] + p[ROWS:] + dot(hi, el_ref[:, c0:c1])) * inv

    mine = pl.multiple_of(r * PIECE, 8)
    theirs = pl.multiple_of(other * PIECE, 8)
    x0 = jnp.concatenate([x_ref[pl.ds(mine, PIECE)], x_ref[pl.ds(theirs, PIECE)]], axis=0) * inv
    x1 = 1.5 * x0 - 0.5 * times(times(x0))
    p = times(x1)
    q = 1.5 * p - 0.5 * times(times(p))
    p = times(q)
    p2 = times(p)
    partner = (c, other)
    fs = [net.slot() for _ in TILES]
    for slot, (c0, c1) in zip(fs, TILES):
        x2 = 1.5 * x1[:, c0:c1] - 0.5 * (1.5 * p[:, c0:c1] - 0.5 * times(p2, c0, c1))
        ii = lax.broadcasted_iota(jnp.int32, (PIECE, c1 - c0), 0)
        jj = lax.broadcasted_iota(jnp.int32, (PIECE, c1 - c0), 1) + c0
        stage[:, c0:c1] = jnp.where(ii + theirs == jj, 0.5, 0.0) - 0.5 * x2[PIECE:]
        net.copy(slot, stage.at[:, c0:c1], out_ref.at[g, :, c0:c1], partner)
        out_ref[g, :, c0:c1] = jnp.where(ii + mine == jj, 0.5, 0.0) - 0.5 * x2[:PIECE]
    for s in net.sent:
        s.wait_send()
    finish()
    for slot, (c0, c1) in zip(fs, TILES):
        net.arrived(slot, out_ref.at[1 - g, :, c0:c1], partner)
    assert net.slots <= SLOTS


def on_device(ncol, hamiltonian_band, margin_factors, neighbour_mask, fermi_level):
    vm = pl.BlockSpec(memory_space=pltpu.VMEM)
    return pl.pallas_call(
        functools.partial(fused, ncol),
        out_shape=jax.ShapeDtypeStruct((2, PIECE, M), F32),
        in_specs=[pl.BlockSpec(memory_space=pltpu.HBM)] * 4,
        out_specs=vm,
        scratch_shapes=[
            pltpu.VMEM((6, 2, 4, 4, 8, B), F32),
            pltpu.VMEM((NC, NC, B, B), F32),
            pltpu.VMEM((M, M), F32),
            pltpu.VMEM((M, PS), F32),
            pltpu.VMEM((M, M), F32),
            pltpu.VMEM((M, M), BF),
            pltpu.VMEM((M, M), BF),
            pltpu.VMEM((PIECE, M), F32),
            pltpu.VMEM((2, SIDE, SIDE, 16, B), F32),
            pltpu.SMEM((2, NC), jnp.int32),
            pltpu.SMEM((1,), F32),
            pltpu.SemaphoreType.DMA((SLOTS,)),
            pltpu.SemaphoreType.DMA((SLOTS,)),
            pltpu.SemaphoreType.DMA((6,)),
            pltpu.SemaphoreType.REGULAR,
            pltpu.SemaphoreType.REGULAR,
        ],
        compiler_params=pltpu.CompilerParams(collective_id=0, has_side_effects=True, vmem_limit_bytes=(107 << 19)),
    )(neighbour_mask, fermi_level, hamiltonian_band, margin_factors)


def solution(mesh):
    in_specs = (P("cols", None, None, None), P("cols", "rep", None), P("cols", None), P())
    return jax.shard_map(
        functools.partial(on_device, mesh.shape["cols"]), mesh=mesh, in_specs=in_specs,
        out_specs=P("cols", "rep", None), check_vma=False)
```

```python
import functools
import jax, jax.numpy as jnp
from jax import lax
from jax.experimental import pallas as pl
from jax.experimental.pallas import tpu as pltpu
from jax.sharding import PartitionSpec as P

B = 128
NC = 5
M = 640
PS = 256
ROWS = 80
PIECE = 40
SIDE = 4
F32 = jnp.float32
BF = jnp.bfloat16
MESH = pl.DeviceIdType.MESH


def split(x):
    hi = x.astype(BF)
    return hi, (x - hi.astype(F32)).astype(BF)


def dot(a, b):
    return jnp.dot(a, b, preferred_element_type=F32)


def dot_nt(a, b):
    return lax.dot_general(a, b, (((1,), (1,)), ((), ())), preferred_element_type=F32)


def dot3(a, b, d=dot):
    (ah, al), (bh, bl) = a, b
    return d(ah, bh) + d(ah, bl) + d(al, bh)


class Net:
    def __init__(self, send, recv):
        self.send, self.recv = send, recv
        self.slots = 0
        self.sent = []

    def slot(self):
        self.slots += 1
        return self.slots - 1

    def copy(self, slot, src, dst, dev):
        c = pltpu.make_async_remote_copy(
            src_ref=src, dst_ref=dst, send_sem=self.send.at[slot], recv_sem=self.recv.at[slot],
            device_id=dev, device_id_type=MESH)
        c.start()
        self.sent.append(c)

    def arrived(self, slot, dst, dev):
        pltpu.make_async_remote_copy(
            src_ref=dst, dst_ref=dst, send_sem=self.send.at[slot], recv_sem=self.recv.at[slot],
            device_id=dev, device_id_type=MESH).wait_recv()


SLOTS = 64
TILES = ((0, 256), (256, 512), (512, 640))
BLOCKS = {
    0: {+1: ((1, 1, 1, 5), (0, 0, 2, 3), (0, 0, 3, 5)), -1: ((0, 4, 0, 3),)},
    1: {+1: ((1, 0, 2, 5),), -1: ((0, 3, 0, 4), (1, 4, 0, 3))},
}
OWN = {0: ((0, 2, 0, 5), (1, 3, 0, 4)), 1: ((1, 2, 0, 5), (0, 1, 1, 5))}
OFFSETS = (0, 1, 3, 2)


def gather(ncol, c, r, g, gd, hb_ref, mf_ref, yb, hbuf, net, loc, near_sem, far_sem, yfar, between):
    y, x = lax.div(r, SIDE), lax.rem(r, SIDE)
    core = lax.rem(c, 2)
    mate = c + 1 - 2 * core
    far = lax.rem(c + ncol - 1 + 2 * core, ncol)

    def dev(col, h, dp):
        if h == 0:
            return (col, y * SIDE + (lax.rem(x + dp + 4, SIDE) if dp else x))
        return (col, (lax.rem(y + dp + 4, SIDE) if dp else y) * SIDE + x)

    def cross(col):
        return [dev(col, h, dp) for h in (0, 1) for dp in OFFSETS if not (dp == 0 and h == 1)]

    def greet(sem, d):
        pl.semaphore_signal(sem, inc=1, device_id=d, device_id_type=MESH)

    barrier = pltpu.get_barrier_semaphore()
    home = c - core

    @pl.when(core == 0)
    def _():
        for d in cross(c)[1:]:
            greet(barrier, d)
        for q in range(SIDE * SIDE):
            greet(barrier, (far, q))

    @pl.when(core == 1)
    def _():
        for d in cross(home):
            greet(barrier, d)
    pl.semaphore_wait(barrier, 13 + 3 * core)

    mine = {0: x, 1: y}

    def at(h, w, n, second, first):
        return yb.at[pl.ds(w, n), h, second, first]

    def own(h):
        return mf_ref.at[:, 8 * h:8 * h + 8]

    w_mate, w_far = 4 * (1 - core), 4 * core
    sl_own = {(h, dp): net.slot() for h in (0, 1) for dp in OFFSETS[1:]}
    sl_mate = {(h, dp): net.slot() for h in (0, 1) for dp in OFFSETS}
    sl_far = [net.slot() for _ in range(SIDE * SIDE)]
    got_far = sl_far[0]
    hs = {(s, i): net.slot() for s in (+1, -1) for i in (0, 1, 2)}

    def needed(to_core, gg):
        return ((0, 2) if gg == 0 else (1, 2)) if to_core == 0 else ((0, 1) if gg == 0 else (0, 2))

    def far_copy(on, q):
        k0, k1 = needed(1 - on, q % 2 if on else q // SIDE % 2)
        return pltpu.make_async_remote_copy(
            src_ref=mf_ref.at[k0:k1], dst_ref=yfar.at[k0:k1, y, x],
            send_sem=net.send.at[sl_far[q]], recv_sem=net.recv.at[got_far],
            device_id=(far, q), device_id_type=MESH)

    def blocks(s, i, k, a, e0, e1, shift=0):
        to = lax.rem(c + ncol + s, ncol)
        return pltpu.make_async_remote_copy(
            src_ref=hb_ref.at[k, e0:e1], dst_ref=hbuf.at[a, e0:e1], send_sem=net.send.at[hs[s, i]],
            recv_sem=net.recv.at[hs[s, i]], device_id=(to, r - shift), device_id_type=MESH)

    def far_blocks(on, op):
        for gg in (0, 1):
            @pl.when(gd == gg)
            def _():
                s = 2 * on - 1
                for i, b in enumerate(BLOCKS[gg][s]):
                    if (s, i) != (+1, 2):
                        op(blocks(s, i, *b))
                if (on, gg) == (1, 1):
                    op(blocks(+1, 2, *BLOCKS[0][+1][2], shift=1))

    def far_sends(on):
        for q in range(SIDE * SIDE):
            far_copy(on, q).start()
        far_blocks(on, lambda d: d.start())

    @pl.when(core == 0)
    def _():
        greet(near_sem, (mate, r))

    @pl.when(core == 1)
    def _():
        for q in range(SIDE * SIDE):
            greet(far_sem, (far, q))
        far_sends(1)
        pl.semaphore_wait(near_sem, 1)
    for dp in (2, 1, 3, 0):
        for h in (0, 1):
            net.copy(sl_mate[h, dp], own(h), at(h, 4 * core, 2, mine[1 - h], mine[h]), dev(mate, h, dp))
            if dp:
                net.copy(sl_own[h, dp], own(h), at(h, 2, 2, mine[1 - h], mine[h]), dev(c, h, dp))
    local = []
    for h in (0, 1):
        l = pltpu.make_async_copy(own(h), at(h, 2, 2, mine[1 - h], mine[h]), loc.at[h])
        l.start()
        local.append(l)
    for gg in (0, 1):
        for on in (0, 1):
            @pl.when((core == on) & (gd == gg))
            def _():
                s = 1 - 2 * on
                for i, b in enumerate(BLOCKS[gg][s]):
                    blocks(s, i, *b).start()

        @pl.when(g == gg)
        def _():
            for i, (k, a, e0, e1) in enumerate(OWN[gg]):
                pltpu.make_async_copy(hb_ref.at[k, e0:e1], hbuf.at[a, e0:e1], loc.at[2 + i]).start()

    start = {0: 2 - 2 * core, 1: w_far}
    half = {0: 2, 1: 1}
    keys = [(u, h, s) for u in (0,) for h in (0, 1) for s in (+1, -1)]
    s2 = {key + (p,): net.slot() for key in keys for p in (0, 1)}
    s2r = {key: net.slot() for key in keys}
    lead = {+1: 0, -1: 1}

    def place(h, dp):
        return lax.rem(mine[h] + 4 - dp, SIDE)

    def along(h, s):
        return dev(c, 1 - h, s)

    def second(h, s):
        return lax.rem(mine[1 - h] + 4 + s, SIDE)

    def rows(u, h, p, q):
        return yb.at[pl.ds(start[u] + p * half[u], half[u]), h, q]

    def send2(u, h):
        for first in (True, False):
            for s in (+1, -1):
                p = lead[s] if first else 1 - lead[s]
                ref = rows(u, h, p, mine[1 - h])
                net.copy(s2[u, h, s, p], ref, ref, along(h, s))

    def relay2(u, h):
        for s in (+1, -1):
            ref = rows(u, h, lead[s], second(h, -s))
            net.arrived(s2[u, h, s, lead[s]], ref, along(h, -s))
            net.copy(s2r[u, h, s], ref, ref, along(h, s))

    def last2(u, h):
        for s in (+1, -1):
            p = 1 - lead[s]
            net.arrived(s2[u, h, s, p], rows(u, h, p, second(h, -s)), along(h, -s))
            net.arrived(s2r[u, h, s], rows(u, h, lead[s], second(h, 2)), along(h, -s))

    def answer(when):
        @pl.when(when)
        def _():
            pl.semaphore_wait(far_sem, SIDE * SIDE)
            far_sends(0)

    for h in (0, 1):
        local[h].wait()
        for dp in OFFSETS:
            if dp:
                net.arrived(sl_own[h, dp], at(h, 2, 2, mine[1 - h], place(h, dp)), along(h, 1))
            net.arrived(sl_mate[h, dp], at(h, w_mate, 2, mine[1 - h], place(h, dp)), along(h, 1))
        send2(0, h)
    answer((core == 0) & (c > 0))
    for h in (0, 1):
        relay2(0, h)
    for h in (0, 1):
        last2(0, h)
    answer(c == 0)

    def far_rows():
        for gg in (0, 1):
            for on in (0, 1):
                @pl.when((core == on) & (g == gg))
                def _():
                    k0, k1 = needed(on, gg)
                    net.arrived(got_far, yfar.at[k0:k1], (far, r))
        for k in (0, 1):
            yb[w_far + k, 0] = yfar[k, :, :, 0:8]
            for p in range(SIDE):
                for q in range(SIDE):
                    yb[w_far + k, 1, p, q] = yfar[k, q, p, 8:16]

    def far_band():
        for gg in (0, 1):
            @pl.when(g == gg)
            def _():
                for s in (+1, -1):
                    for i, b in enumerate(BLOCKS[gg][s]):
                        blocks(s, i, *b).wait_recv()
                for i, (k, a, e0, e1) in enumerate(OWN[gg]):
                    pltpu.make_async_copy(hb_ref.at[k, e0:e1], hbuf.at[a, e0:e1], loc.at[2 + i]).wait()
        between()

    def finish():
        for on in (0, 1):
            @pl.when(core == on)
            def _():
                for q in range(SIDE * SIDE):
                    far_copy(on, q).wait_send()
                far_blocks(on, lambda d: d.wait_send())
                for gg in (0, 1):
                    @pl.when(gd == gg)
                    def _():
                        s = 1 - 2 * on
                        for i, b in enumerate(BLOCKS[gg][s]):
                            blocks(s, i, *b).wait_send()
    return far_rows, far_band, finish


def cat3l(a, b):
    return jnp.concatenate([a, b, a], axis=1)


def vsum(e):
    return jnp.sum(e.reshape(-1, 8, e.shape[1]), axis=0)


def cdot(a, b):
    return dot(cat3l(*a), jnp.concatenate([b[0], b[0], b[1]], axis=0))


def fused(ncol, mask_hbm, fermi_hbm, hb_ref, mf_ref, out_ref, yb, hbuf, h_ref, yt_ref, x_ref, eh_ref, el_ref,
          stage, yfar, mask_ref, fermi_ref, send, recv, loc, near_sem, far_sem):
    c = lax.axis_index("cols")
    r = lax.axis_index("rep")
    y, x = lax.div(r, SIDE), lax.rem(r, SIDE)
    core = lax.rem(c, 2)
    g = lax.rem(x * (1 - core) + y * core, 2)
    gd = lax.rem(x * core + y * (1 - core), 2)
    other = r + (1 - 2 * g) * (1 + 3 * core)
    small = [pltpu.make_async_copy(mask_hbm, mask_ref, loc.at[4]), pltpu.make_async_copy(fermi_hbm, fermi_ref, loc.at[5])]
    for s in small:
        s.start()
    net = Net(send, recv)
    mask = []

    def between():
        for a in range(NC):
            for b in range(NC):
                sl = (slice(a * B, (a + 1) * B), slice(b * B, (b + 1) * B))
                if abs(a - b) <= 2:
                    w = 0.5 * mask[a] * mask[b]
                    h_ref[sl] = (hbuf[b, a - b + 2] + hbuf[a, b - a + 2].T) * w
                else:
                    h_ref[sl] = jnp.zeros((B, B), F32)

    far_rows, far_band, finish = gather(
        ncol, c, r, g, gd, hb_ref, mf_ref, yb, hbuf, net, loc, near_sem, far_sem, yfar, between)
    for o in small:
        o.wait()
    mask.extend(mask_ref[g, a].astype(F32) for a in range(NC))
    far_rows()
    mu = fermi_ref[0]
    ys = [yb[g + a].reshape(PS, B) * mask[a] for a in range(NC)]
    for a in range(NC):
        yt_ref[a * B:(a + 1) * B, :] = ys[a].T
    yt = split(yt_ref[...])
    yy = split(jnp.concatenate(ys, axis=1))
    eye = lax.broadcasted_iota(jnp.int32, (PS, PS), 0) == lax.broadcasted_iota(jnp.int32, (PS, PS), 1)
    k = cdot(yy, yt)
    ks = split(k)
    far_band()
    pt = cdot(split(h_ref[...]), yt)
    k2 = cdot(ks, ks)
    n = cdot(yy, split(pt))
    k3 = cdot(ks, split(k2))
    one = jnp.ones((1, 1), F32)
    sumsq = M * one + jnp.sum(vsum(jnp.where(eye, 2.0 * k, 0.0) + k * k), keepdims=True)
    cs = 2.0 * jnp.sqrt(sumsq / M)
    al = 1.0 / cs
    t = 0.5 * (3.0 - al)
    u = 0.5 * (3.0 - al * t * t)
    b0 = al * t * (t - al)
    b1 = al * al * (0.25 * al - t)
    b2 = 0.25 * al * al * al
    rs = lax.rsqrt(cs)
    q0 = (-0.5 * t * b0 - 0.5 * al * u) * rs
    q1 = (-0.5 * t * b1 + 0.25 * al * b0) * rs
    q2 = (-0.5 * t * b2 + 0.25 * al * b1) * rs
    q3 = (0.25 * al * b2) * rs
    a0 = t * u * rs
    rm = q1 * k + q2 * k2 + q3 * k3 + jnp.where(eye, q0, 0.0)
    rms = split(rm)
    rn = split(0.5 * cdot(rms, split(n)))
    both = cdot(yt, (jnp.concatenate([rms[0], rn[0]], axis=1), jnp.concatenate([rms[1], rn[1]], axis=1)))
    vts = split(both[:, :PS])
    pts = split(a0 * pt + both[:, PS:])
    a2 = a0 * a0
    lh, ll = (jnp.concatenate([pts[i], vts[i]], axis=1) for i in (0, 1))
    rh, rl = (jnp.concatenate([vts[i], pts[i]], axis=1) for i in (0, 1))
    lcat = cat3l(lh, ll)
    rcat = jnp.concatenate([rh, rh, rl], axis=1)

    def put(e, p, q):
        eh_ref[p:p + B, q:q + B], el_ref[p:p + B, q:q + B] = split(e)
        x_ref[p:p + B, q:q + B] = e

    total = jnp.zeros((8, B), F32)
    eye = lax.broadcasted_iota(jnp.int32, (B, B), 0) == lax.broadcasted_iota(jnp.int32, (B, B), 1)
    for c0, c1 in TILES:
        e = dot_nt(lcat[c0:], rcat[c0:c1]) + a2 * h_ref[c0:, c0:c1]
        for p in range(c0, M, B):
            for q in range(c0, c1, B):
                block = e[p - c0:p - c0 + B, q - c0:q - c0 + B]
                if p == q:
                    block = block - jnp.where(eye, mu, 0.0)
                if p >= c1:
                    total = total + 2.0 * vsum(block * block)
                    put(block.T, q, p)
                else:
                    total = total + vsum(block * block)
                put(block, p, q)
    acc = jnp.sum(total, keepdims=True)
    inv = 1.0 / (2.0 * jnp.sqrt(acc / M + 1e-5))

    def times(v, c0=0, c1=M):
        hi, lo = split(v)
        p = dot(jnp.concatenate([hi, lo], axis=0), eh_ref[:, c0:c1])
        return (p[:ROWS] + p[ROWS:] + dot(hi, el_ref[:, c0:c1])) * inv

    mine = pl.multiple_of(r * PIECE, 8)
    theirs = pl.multiple_of(other * PIECE, 8)
    x0 = jnp.concatenate([x_ref[pl.ds(mine, PIECE)], x_ref[pl.ds(theirs, PIECE)]], axis=0) * inv
    x1 = 1.5 * x0 - 0.5 * times(times(x0))
    p = times(x1)
    q = 1.5 * p - 0.5 * times(times(p))
    p = times(q)
    p2 = times(p)
    partner = (c, other)
    fs = [net.slot() for _ in TILES]
    for slot, (c0, c1) in zip(fs, TILES):
        x2 = 1.5 * x1[:, c0:c1] - 0.5 * (1.5 * p[:, c0:c1] - 0.5 * times(p2, c0, c1))
        ii = lax.broadcasted_iota(jnp.int32, (PIECE, c1 - c0), 0)
        jj = lax.broadcasted_iota(jnp.int32, (PIECE, c1 - c0), 1) + c0
        stage[:, c0:c1] = jnp.where(ii + theirs == jj, 0.5, 0.0) - 0.5 * x2[PIECE:]
        net.copy(slot, stage.at[:, c0:c1], out_ref.at[g, :, c0:c1], partner)
        out_ref[g, :, c0:c1] = jnp.where(ii + mine == jj, 0.5, 0.0) - 0.5 * x2[:PIECE]
    for s in net.sent:
        s.wait_send()
    finish()
    for slot, (c0, c1) in zip(fs, TILES):
        net.arrived(slot, out_ref.at[1 - g, :, c0:c1], partner)
    assert net.slots <= SLOTS


def on_device(ncol, hamiltonian_band, margin_factors, neighbour_mask, fermi_level):
    vm = pl.BlockSpec(memory_space=pltpu.VMEM)
    return pl.pallas_call(
        functools.partial(fused, ncol),
        out_shape=jax.ShapeDtypeStruct((2, PIECE, M), F32),
        in_specs=[pl.BlockSpec(memory_space=pltpu.HBM)] * 4,
        out_specs=vm,
        scratch_shapes=[
            pltpu.VMEM((6, 2, 4, 4, 8, B), F32),
            pltpu.VMEM((NC, NC, B, B), F32),
            pltpu.VMEM((M, M), F32),
            pltpu.VMEM((M, PS), F32),
            pltpu.VMEM((M, M), F32),
            pltpu.VMEM((M, M), BF),
            pltpu.VMEM((M, M), BF),
            pltpu.VMEM((PIECE, M), F32),
            pltpu.VMEM((2, SIDE, SIDE, 16, B), F32),
            pltpu.SMEM((2, NC), jnp.int32),
            pltpu.SMEM((1,), F32),
            pltpu.SemaphoreType.DMA((SLOTS,)),
            pltpu.SemaphoreType.DMA((SLOTS,)),
            pltpu.SemaphoreType.DMA((6,)),
            pltpu.SemaphoreType.REGULAR,
            pltpu.SemaphoreType.REGULAR,
        ],
        compiler_params=pltpu.CompilerParams(collective_id=0, has_side_effects=True, vmem_limit_bytes=(107 << 19)),
    )(neighbour_mask, fermi_level, hamiltonian_band, margin_factors)


def solution(mesh):
    in_specs = (P("cols", None, None, None), P("cols", "rep", None), P("cols", None), P())
    return jax.shard_map(
        functools.partial(on_device, mesh.shape["cols"]), mesh=mesh, in_specs=in_specs,
        out_specs=P("cols", "rep", None), check_vma=False)
```

```python
import functools
import jax, jax.numpy as jnp
from jax import lax
from jax.experimental import pallas as pl
from jax.experimental.pallas import tpu as pltpu
from jax.sharding import PartitionSpec as P

B = 128
NC = 5
M = 640
PS = 256
ROWS = 80
PIECE = 40
SIDE = 4
F32 = jnp.float32
BF = jnp.bfloat16
MESH = pl.DeviceIdType.MESH


def split(x):
    hi = x.astype(BF)
    return hi, (x - hi.astype(F32)).astype(BF)


def dot(a, b):
    return jnp.dot(a, b, preferred_element_type=F32)


def dot_nt(a, b):
    return lax.dot_general(a, b, (((1,), (1,)), ((), ())), preferred_element_type=F32)


def dot3(a, b, d=dot):
    (ah, al), (bh, bl) = a, b
    return d(ah, bh) + d(ah, bl) + d(al, bh)


class Net:
    def __init__(self, send, recv):
        self.send, self.recv = send, recv
        self.slots = 0
        self.sent = []

    def slot(self):
        self.slots += 1
        return self.slots - 1

    def copy(self, slot, src, dst, dev):
        c = pltpu.make_async_remote_copy(
            src_ref=src, dst_ref=dst, send_sem=self.send.at[slot], recv_sem=self.recv.at[slot],
            device_id=dev, device_id_type=MESH)
        c.start()
        self.sent.append(c)

    def arrived(self, slot, dst, dev):
        pltpu.make_async_remote_copy(
            src_ref=dst, dst_ref=dst, send_sem=self.send.at[slot], recv_sem=self.recv.at[slot],
            device_id=dev, device_id_type=MESH).wait_recv()


SLOTS = 64
TILES = ((0, 256), (256, 512), (512, 640))
BLOCKS = {
    0: {+1: ((1, 1, 1, 5), (0, 0, 2, 3), (0, 0, 3, 5)), -1: ((0, 4, 0, 3),)},
    1: {+1: ((1, 0, 2, 5),), -1: ((0, 3, 0, 4), (1, 4, 2, 3), (1, 4, 0, 2))},
}
OWN = {0: ((0, 2, 0, 5), (1, 3, 0, 4)), 1: ((1, 2, 0, 5), (0, 1, 1, 5))}
OFFSETS = (0, 1, 3, 2)


def gather(ncol, c, r, g, gd, hb_ref, mf_ref, yb, hbuf, net, loc, near_sem, far_sem, yfar, between):
    y, x = lax.div(r, SIDE), lax.rem(r, SIDE)
    core = lax.rem(c, 2)
    mate = c + 1 - 2 * core
    far = lax.rem(c + ncol - 1 + 2 * core, ncol)

    def dev(col, h, dp):
        if h == 0:
            return (col, y * SIDE + (lax.rem(x + dp + 4, SIDE) if dp else x))
        return (col, (lax.rem(y + dp + 4, SIDE) if dp else y) * SIDE + x)

    def cross(col):
        return [dev(col, h, dp) for h in (0, 1) for dp in OFFSETS if not (dp == 0 and h == 1)]

    def greet(sem, d):
        pl.semaphore_signal(sem, inc=1, device_id=d, device_id_type=MESH)

    barrier = pltpu.get_barrier_semaphore()
    home = c - core

    @pl.when(core == 0)
    def _():
        for d in cross(c)[1:]:
            greet(barrier, d)
        for q in range(SIDE * SIDE):
            greet(barrier, (far, q))

    @pl.when(core == 1)
    def _():
        for d in cross(home):
            greet(barrier, d)

    inner = core * (1 - lax.div(c + 1, ncol))

    @pl.when(inner == 1)
    def _():
        for q in range(1, SIDE * SIDE):
            greet(barrier, (c, lax.rem(r + q, SIDE * SIDE)))
    pl.semaphore_wait(barrier, 13 + 3 * core + 15 * inner)

    mine = {0: x, 1: y}

    def at(h, w, n, second, first):
        return yb.at[pl.ds(w, n), h, second, first]

    def own(h):
        return mf_ref.at[:, 8 * h:8 * h + 8]

    w_mate, w_far = 4 * (1 - core), 4 * core
    sl_own = {(h, dp): net.slot() for h in (0, 1) for dp in OFFSETS[1:]}
    sl_mate = {(h, dp): net.slot() for h in (0, 1) for dp in OFFSETS}
    sl_far = [net.slot() for _ in range(SIDE * SIDE)]
    got_far = sl_far[0]
    hs = {(s, i): net.slot() for s in (+1, -1) for i in (0, 1, 2)}

    def needed(to_core, gg):
        return ((0, 2) if gg == 0 else (1, 2)) if to_core == 0 else ((0, 1) if gg == 0 else (0, 2))

    def far_copy(on, q):
        k0, k1 = needed(1 - on, q % 2 if on else q // SIDE % 2)
        return pltpu.make_async_remote_copy(
            src_ref=mf_ref.at[k0:k1], dst_ref=yfar.at[k0:k1, y, x],
            send_sem=net.send.at[sl_far[q]], recv_sem=net.recv.at[got_far],
            device_id=(far, q), device_id_type=MESH)

    def blocks(s, i, k, a, e0, e1, shift=0):
        to = lax.rem(c + ncol + s, ncol)
        return pltpu.make_async_remote_copy(
            src_ref=hb_ref.at[k, e0:e1], dst_ref=hbuf.at[a, e0:e1], send_sem=net.send.at[hs[s, i]],
            recv_sem=net.recv.at[hs[s, i]], device_id=(to, r - shift), device_id_type=MESH)

    def far_blocks(on, op):
        for gg in (0, 1):
            @pl.when(gd == gg)
            def _():
                s = 2 * on - 1
                for i, b in enumerate(BLOCKS[gg][s]):
                    if i < 2:
                        op(blocks(s, i, *b))
                if (on, gg) == (1, 1):
                    op(blocks(+1, 2, *BLOCKS[0][+1][2], shift=1))
                if (on, gg) == (0, 0):
                    op(blocks(-1, 2, *BLOCKS[1][-1][2], shift=-SIDE))

    def far_sends(on):
        for q in range(SIDE * SIDE):
            far_copy(on, q).start()
        far_blocks(on, lambda d: d.start())

    @pl.when(core == 0)
    def _():
        greet(near_sem, (mate, r))

    @pl.when(core == 1)
    def _():
        greet(far_sem, (far, r))

        @pl.when(inner == 0)
        def _():
            for q in range(1, SIDE * SIDE):
                greet(far_sem, (far, lax.rem(r + q, SIDE * SIDE)))
        far_sends(1)
        pl.semaphore_wait(near_sem, 1)
    for dp in (2, 1, 3, 0):
        for h in (0, 1):
            net.copy(sl_mate[h, dp], own(h), at(h, 4 * core, 2, mine[1 - h], mine[h]), dev(mate, h, dp))
            if dp:
                net.copy(sl_own[h, dp], own(h), at(h, 2, 2, mine[1 - h], mine[h]), dev(c, h, dp))
    local = []
    for h in (0, 1):
        l = pltpu.make_async_copy(own(h), at(h, 2, 2, mine[1 - h], mine[h]), loc.at[h])
        l.start()
        local.append(l)
    for gg in (0, 1):
        for on in (0, 1):
            @pl.when((core == on) & (gd == gg))
            def _():
                s = 1 - 2 * on
                for i, b in enumerate(BLOCKS[gg][s]):
                    blocks(s, i, *b).start()

        @pl.when(g == gg)
        def _():
            for i, (k, a, e0, e1) in enumerate(OWN[gg]):
                pltpu.make_async_copy(hb_ref.at[k, e0:e1], hbuf.at[a, e0:e1], loc.at[2 + i]).start()

    start = {0: 2 - 2 * core, 1: w_far}
    half = {0: 2, 1: 1}
    keys = [(u, h, s) for u in (0,) for h in (0, 1) for s in (+1, -1)]
    s2 = {key + (p,): net.slot() for key in keys for p in (0, 1)}
    s2r = {key: net.slot() for key in keys}
    lead = {+1: 0, -1: 1}

    def place(h, dp):
        return lax.rem(mine[h] + 4 - dp, SIDE)

    def along(h, s):
        return dev(c, 1 - h, s)

    def second(h, s):
        return lax.rem(mine[1 - h] + 4 + s, SIDE)

    def rows(u, h, p, q):
        return yb.at[pl.ds(start[u] + p * half[u], half[u]), h, q]

    def send2(u, h):
        for first in (True, False):
            for s in (+1, -1):
                p = lead[s] if first else 1 - lead[s]
                ref = rows(u, h, p, mine[1 - h])
                net.copy(s2[u, h, s, p], ref, ref, along(h, s))

    def relay2(u, h):
        for s in (+1, -1):
            ref = rows(u, h, lead[s], second(h, -s))
            net.arrived(s2[u, h, s, lead[s]], ref, along(h, -s))
            net.copy(s2r[u, h, s], ref, ref, along(h, s))

    def last2(u, h):
        for s in (+1, -1):
            p = 1 - lead[s]
            net.arrived(s2[u, h, s, p], rows(u, h, p, second(h, -s)), along(h, -s))
            net.arrived(s2r[u, h, s], rows(u, h, lead[s], second(h, 2)), along(h, -s))

    def answer(when, answers):
        @pl.when(when)
        def _():
            pl.semaphore_wait(far_sem, answers)
            far_sends(0)

    answer((core == 0) & (c > 0), 1)
    for h in (0, 1):
        local[h].wait()
        for dp in OFFSETS:
            if dp:
                net.arrived(sl_own[h, dp], at(h, 2, 2, mine[1 - h], place(h, dp)), along(h, 1))
            net.arrived(sl_mate[h, dp], at(h, w_mate, 2, mine[1 - h], place(h, dp)), along(h, 1))
        send2(0, h)
    for h in (0, 1):
        relay2(0, h)
    for h in (0, 1):
        last2(0, h)
    answer(c == 0, SIDE * SIDE)

    def far_rows():
        for gg in (0, 1):
            for on in (0, 1):
                @pl.when((core == on) & (g == gg))
                def _():
                    k0, k1 = needed(on, gg)
                    net.arrived(got_far, yfar.at[k0:k1], (far, r))
        for k in (0, 1):
            yb[w_far + k, 0] = yfar[k, :, :, 0:8]
            for p in range(SIDE):
                for q in range(SIDE):
                    yb[w_far + k, 1, p, q] = yfar[k, q, p, 8:16]

    def far_band():
        for gg in (0, 1):
            @pl.when(g == gg)
            def _():
                for s in (+1, -1):
                    for i, b in enumerate(BLOCKS[gg][s]):
                        blocks(s, i, *b).wait_recv()
                for i, (k, a, e0, e1) in enumerate(OWN[gg]):
                    pltpu.make_async_copy(hb_ref.at[k, e0:e1], hbuf.at[a, e0:e1], loc.at[2 + i]).wait()
        between()

    def finish():
        for on in (0, 1):
            @pl.when(core == on)
            def _():
                for q in range(SIDE * SIDE):
                    far_copy(on, q).wait_send()
                far_blocks(on, lambda d: d.wait_send())
                for gg in (0, 1):
                    @pl.when(gd == gg)
                    def _():
                        s = 1 - 2 * on
                        for i, b in enumerate(BLOCKS[gg][s]):
                            blocks(s, i, *b).wait_send()
    return far_rows, far_band, finish


def cat3l(a, b):
    return jnp.concatenate([a, b, a], axis=1)


def vsum(e):
    return jnp.sum(e.reshape(-1, 8, e.shape[1]), axis=0)


def cdot(a, b):
    return dot(cat3l(*a), jnp.concatenate([b[0], b[0], b[1]], axis=0))


def fused(ncol, mask_hbm, fermi_hbm, hb_ref, mf_ref, out_ref, yb, hbuf, h_ref, yt_ref, x_ref, eh_ref, el_ref,
          stage, yfar, mask_ref, fermi_ref, send, recv, loc, near_sem, far_sem):
    c = lax.axis_index("cols")
    r = lax.axis_index("rep")
    y, x = lax.div(r, SIDE), lax.rem(r, SIDE)
    core = lax.rem(c, 2)
    g = lax.rem(x * (1 - core) + y * core, 2)
    gd = lax.rem(x * core + y * (1 - core), 2)
    other = r + (1 - 2 * g) * (1 + 3 * core)
    small = [pltpu.make_async_copy(mask_hbm, mask_ref, loc.at[4]), pltpu.make_async_copy(fermi_hbm, fermi_ref, loc.at[5])]
    for s in small:
        s.start()
    net = Net(send, recv)
    mask = []

    def between():
        for a in range(NC):
            for b in range(NC):
                sl = (slice(a * B, (a + 1) * B), slice(b * B, (b + 1) * B))
                if abs(a - b) <= 2:
                    w = 0.5 * mask[a] * mask[b]
                    h_ref[sl] = (hbuf[b, a - b + 2] + hbuf[a, b - a + 2].T) * w
                else:
                    h_ref[sl] = jnp.zeros((B, B), F32)

    far_rows, far_band, finish = gather(
        ncol, c, r, g, gd, hb_ref, mf_ref, yb, hbuf, net, loc, near_sem, far_sem, yfar, between)
    for o in small:
        o.wait()
    mask.extend(mask_ref[g, a].astype(F32) for a in range(NC))
    far_rows()
    mu = fermi_ref[0]
    ys = [yb[g + a].reshape(PS, B) * mask[a] for a in range(NC)]
    for a in range(NC):
        yt_ref[a * B:(a + 1) * B, :] = ys[a].T
    yt = split(yt_ref[...])
    yy = split(jnp.concatenate(ys, axis=1))
    eye = lax.broadcasted_iota(jnp.int32, (PS, PS), 0) == lax.broadcasted_iota(jnp.int32, (PS, PS), 1)
    k = cdot(yy, yt)
    ks = split(k)
    far_band()
    pt = cdot(split(h_ref[...]), yt)
    k2 = cdot(ks, ks)
    n = cdot(yy, split(pt))
    k3 = cdot(ks, split(k2))
    one = jnp.ones((1, 1), F32)
    sumsq = M * one + jnp.sum(vsum(jnp.where(eye, 2.0 * k, 0.0) + k * k), keepdims=True)
    cs = 2.0 * jnp.sqrt(sumsq / M)
    al = 1.0 / cs
    t = 0.5 * (3.0 - al)
    u = 0.5 * (3.0 - al * t * t)
    b0 = al * t * (t - al)
    b1 = al * al * (0.25 * al - t)
    b2 = 0.25 * al * al * al
    rs = lax.rsqrt(cs)
    q0 = (-0.5 * t * b0 - 0.5 * al * u) * rs
    q1 = (-0.5 * t * b1 + 0.25 * al * b0) * rs
    q2 = (-0.5 * t * b2 + 0.25 * al * b1) * rs
    q3 = (0.25 * al * b2) * rs
    a0 = t * u * rs
    rm = q1 * k + q2 * k2 + q3 * k3 + jnp.where(eye, q0, 0.0)
    rms = split(rm)
    rn = split(0.5 * cdot(rms, split(n)))
    both = cdot(yt, (jnp.concatenate([rms[0], rn[0]], axis=1), jnp.concatenate([rms[1], rn[1]], axis=1)))
    vts = split(both[:, :PS])
    pts = split(a0 * pt + both[:, PS:])
    a2 = a0 * a0
    lh, ll = (jnp.concatenate([pts[i], vts[i]], axis=1) for i in (0, 1))
    rh, rl = (jnp.concatenate([vts[i], pts[i]], axis=1) for i in (0, 1))
    lcat = cat3l(lh, ll)
    rcat = jnp.concatenate([rh, rh, rl], axis=1)

    def put(e, p, q):
        eh_ref[p:p + B, q:q + B], el_ref[p:p + B, q:q + B] = split(e)
        x_ref[p:p + B, q:q + B] = e

    total = jnp.zeros((8, B), F32)
    eye = lax.broadcasted_iota(jnp.int32, (B, B), 0) == lax.broadcasted_iota(jnp.int32, (B, B), 1)
    for c0, c1 in TILES:
        e = dot_nt(lcat[c0:], rcat[c0:c1]) + a2 * h_ref[c0:, c0:c1]
        for p in range(c0, M, B):
            for q in range(c0, c1, B):
                block = e[p - c0:p - c0 + B, q - c0:q - c0 + B]
                if p == q:
                    block = block - jnp.where(eye, mu, 0.0)
                if p >= c1:
                    total = total + 2.0 * vsum(block * block)
                    put(block.T, q, p)
                else:
                    total = total + vsum(block * block)
                put(block, p, q)
    acc = jnp.sum(total, keepdims=True)
    inv = 1.0 / (2.0 * jnp.sqrt(acc / M + 1e-5))

    def times(v, c0=0, c1=M):
        hi, lo = split(v)
        p = dot(jnp.concatenate([hi, lo], axis=0), eh_ref[:, c0:c1])
        return (p[:ROWS] + p[ROWS:] + dot(hi, el_ref[:, c0:c1])) * inv

    mine = pl.multiple_of(r * PIECE, 8)
    theirs = pl.multiple_of(other * PIECE, 8)
    x0 = jnp.concatenate([x_ref[pl.ds(mine, PIECE)], x_ref[pl.ds(theirs, PIECE)]], axis=0) * inv
    x1 = 1.5 * x0 - 0.5 * times(times(x0))
    p = times(x1)
    q = 1.5 * p - 0.5 * times(times(p))
    p = times(q)
    p2 = times(p)
    partner = (c, other)
    fs = [net.slot() for _ in TILES]
    for slot, (c0, c1) in zip(fs, TILES):
        x2 = 1.5 * x1[:, c0:c1] - 0.5 * (1.5 * p[:, c0:c1] - 0.5 * times(p2, c0, c1))
        ii = lax.broadcasted_iota(jnp.int32, (PIECE, c1 - c0), 0)
        jj = lax.broadcasted_iota(jnp.int32, (PIECE, c1 - c0), 1) + c0
        stage[:, c0:c1] = jnp.where(ii + theirs == jj, 0.5, 0.0) - 0.5 * x2[PIECE:]
        net.copy(slot, stage.at[:, c0:c1], out_ref.at[g, :, c0:c1], partner)
        out_ref[g, :, c0:c1] = jnp.where(ii + mine == jj, 0.5, 0.0) - 0.5 * x2[:PIECE]
    for s in net.sent:
        s.wait_send()
    finish()
    for slot, (c0, c1) in zip(fs, TILES):
        net.arrived(slot, out_ref.at[1 - g, :, c0:c1], partner)
    assert net.slots <= SLOTS


def on_device(ncol, hamiltonian_band, margin_factors, neighbour_mask, fermi_level):
    vm = pl.BlockSpec(memory_space=pltpu.VMEM)
    return pl.pallas_call(
        functools.partial(fused, ncol),
        out_shape=jax.ShapeDtypeStruct((2, PIECE, M), F32),
        in_specs=[pl.BlockSpec(memory_space=pltpu.HBM)] * 4,
        out_specs=vm,
        scratch_shapes=[
            pltpu.VMEM((6, 2, 4, 4, 8, B), F32),
            pltpu.VMEM((NC, NC, B, B), F32),
            pltpu.VMEM((M, M), F32),
            pltpu.VMEM((M, PS), F32),
            pltpu.VMEM((M, M), F32),
            pltpu.VMEM((M, M), BF),
            pltpu.VMEM((M, M), BF),
            pltpu.VMEM((PIECE, M), F32),
            pltpu.VMEM((2, SIDE, SIDE, 16, B), F32),
            pltpu.SMEM((2, NC), jnp.int32),
            pltpu.SMEM((1,), F32),
            pltpu.SemaphoreType.DMA((SLOTS,)),
            pltpu.SemaphoreType.DMA((SLOTS,)),
            pltpu.SemaphoreType.DMA((6,)),
            pltpu.SemaphoreType.REGULAR,
            pltpu.SemaphoreType.REGULAR,
        ],
        compiler_params=pltpu.CompilerParams(collective_id=0, has_side_effects=True, vmem_limit_bytes=(107 << 19)),
    )(neighbour_mask, fermi_level, hamiltonian_band, margin_factors)


def solution(mesh):
    in_specs = (P("cols", None, None, None), P("cols", "rep", None), P("cols", None), P())
    return jax.shard_map(
        functools.partial(on_device, mesh.shape["cols"]), mesh=mesh, in_specs=in_specs,
        out_specs=P("cols", "rep", None), check_vma=False)
```

```python
import functools
import jax, jax.numpy as jnp
from jax import lax
from jax.experimental import pallas as pl
from jax.experimental.pallas import tpu as pltpu
from jax.sharding import PartitionSpec as P

B = 128
NC = 5
M = 640
PS = 256
ROWS = 80
PIECE = 40
SIDE = 4
F32 = jnp.float32
BF = jnp.bfloat16
MESH = pl.DeviceIdType.MESH


def split(x):
    hi = x.astype(BF)
    return hi, (x - hi.astype(F32)).astype(BF)


def dot(a, b):
    return jnp.dot(a, b, preferred_element_type=F32)


def dot_nt(a, b):
    return lax.dot_general(a, b, (((1,), (1,)), ((), ())), preferred_element_type=F32)


def dot3(a, b, d=dot):
    (ah, al), (bh, bl) = a, b
    return d(ah, bh) + d(ah, bl) + d(al, bh)


class Net:
    def __init__(self, send, recv):
        self.send, self.recv = send, recv
        self.slots = 0
        self.sent = []

    def slot(self):
        self.slots += 1
        return self.slots - 1

    def copy(self, slot, src, dst, dev):
        c = pltpu.make_async_remote_copy(
            src_ref=src, dst_ref=dst, send_sem=self.send.at[slot], recv_sem=self.recv.at[slot],
            device_id=dev, device_id_type=MESH)
        c.start()
        self.sent.append(c)

    def arrived(self, slot, dst, dev):
        pltpu.make_async_remote_copy(
            src_ref=dst, dst_ref=dst, send_sem=self.send.at[slot], recv_sem=self.recv.at[slot],
            device_id=dev, device_id_type=MESH).wait_recv()


SLOTS = 64
TILES = ((0, 256), (256, 512), (512, 640))
BLOCKS = {
    0: {+1: ((1, 1, 1, 5), (0, 0, 2, 3), (0, 0, 3, 5)), -1: ((0, 4, 0, 3),)},
    1: {+1: ((1, 0, 2, 5),), -1: ((0, 3, 0, 4), (1, 4, 2, 3), (1, 4, 0, 2))},
}
OWN = {0: ((0, 2, 0, 5), (1, 3, 0, 4)), 1: ((1, 2, 0, 5), (0, 1, 1, 5))}
OFFSETS = (0, 1, 3, 2)


def gather(ncol, c, r, g, gd, hb_ref, mf_ref, yb, hbuf, net, loc, near_sem, far_sem, yfar, between):
    y, x = lax.div(r, SIDE), lax.rem(r, SIDE)
    core = lax.rem(c, 2)
    mate = c + 1 - 2 * core
    far = lax.rem(c + ncol - 1 + 2 * core, ncol)

    def dev(col, h, dp):
        if h == 0:
            return (col, y * SIDE + (lax.rem(x + dp + 4, SIDE) if dp else x))
        return (col, (lax.rem(y + dp + 4, SIDE) if dp else y) * SIDE + x)

    def cross(col):
        return [dev(col, h, dp) for h in (0, 1) for dp in OFFSETS if not (dp == 0 and h == 1)]

    def greet(sem, d):
        pl.semaphore_signal(sem, inc=1, device_id=d, device_id_type=MESH)

    barrier = pltpu.get_barrier_semaphore()
    home = c - core

    @pl.when(core == 0)
    def _():
        for d in cross(c)[1:]:
            greet(barrier, d)
        for q in range(SIDE * SIDE):
            greet(barrier, (far, q))

    @pl.when(core == 1)
    def _():
        for d in cross(home):
            greet(barrier, d)

    inner = core * (1 - lax.div(c + 1, ncol))

    @pl.when(inner == 1)
    def _():
        for q in range(1, SIDE * SIDE):
            greet(barrier, (c, lax.rem(r + q, SIDE * SIDE)))
    pl.semaphore_wait(barrier, 13 + 3 * core + 15 * inner)

    mine = {0: x, 1: y}

    def at(h, w, n, second, first):
        return yb.at[pl.ds(w, n), h, second, first]

    def own(h):
        return mf_ref.at[:, 8 * h:8 * h + 8]

    w_mate, w_far = 4 * (1 - core), 4 * core
    sl_own = {(h, dp): net.slot() for h in (0, 1) for dp in OFFSETS[1:]}
    sl_mate = {(h, dp): net.slot() for h in (0, 1) for dp in OFFSETS}
    sl_far = [net.slot() for _ in range(SIDE * SIDE)]
    got_far = sl_far[0]
    hs = {(s, i): net.slot() for s in (+1, -1) for i in (0, 1, 2)}

    def needed(to_core, gg):
        return ((0, 2) if gg == 0 else (1, 2)) if to_core == 0 else ((0, 1) if gg == 0 else (0, 2))

    def far_copy(on, q):
        k0, k1 = needed(1 - on, q // SIDE % 2 if on else q % 2)
        return pltpu.make_async_remote_copy(
            src_ref=mf_ref.at[k0:k1], dst_ref=yfar.at[k0:k1, y, x],
            send_sem=net.send.at[sl_far[q]], recv_sem=net.recv.at[got_far],
            device_id=(far, q), device_id_type=MESH)

    def blocks(s, i, k, a, e0, e1, shift=0):
        to = lax.rem(c + ncol + s, ncol)
        return pltpu.make_async_remote_copy(
            src_ref=hb_ref.at[k, e0:e1], dst_ref=hbuf.at[a, e0:e1], send_sem=net.send.at[hs[s, i]],
            recv_sem=net.recv.at[hs[s, i]], device_id=(to, r - shift), device_id_type=MESH)

    def far_blocks(on, op):
        for gg in (0, 1):
            @pl.when(gd == gg)
            def _():
                s = 2 * on - 1
                for i, b in enumerate(BLOCKS[gg][s]):
                    if i < 2:
                        op(blocks(s, i, *b))
                if (on, gg) == (1, 1):
                    op(blocks(+1, 2, *BLOCKS[0][+1][2], shift=SIDE))
                if (on, gg) == (0, 0):
                    op(blocks(-1, 2, *BLOCKS[1][-1][2], shift=-1))

    def far_sends(on):
        for q in range(SIDE * SIDE):
            far_copy(on, q).start()
        far_blocks(on, lambda d: d.start())

    @pl.when(core == 0)
    def _():
        greet(near_sem, (mate, r))

    @pl.when(core == 1)
    def _():
        greet(far_sem, (far, r))

        @pl.when(inner == 0)
        def _():
            for q in range(1, SIDE * SIDE):
                greet(far_sem, (far, lax.rem(r + q, SIDE * SIDE)))
        far_sends(1)
        pl.semaphore_wait(near_sem, 1)
    for dp in (2, 1, 3, 0):
        for h in (0, 1):
            net.copy(sl_mate[h, dp], own(h), at(h, 4 * core, 2, mine[1 - h], mine[h]), dev(mate, h, dp))
            if dp:
                net.copy(sl_own[h, dp], own(h), at(h, 2, 2, mine[1 - h], mine[h]), dev(c, h, dp))
    local = []
    for h in (0, 1):
        l = pltpu.make_async_copy(own(h), at(h, 2, 2, mine[1 - h], mine[h]), loc.at[h])
        l.start()
        local.append(l)
    for gg in (0, 1):
        for on in (0, 1):
            @pl.when((core == on) & (gd == gg))
            def _():
                s = 1 - 2 * on
                for i, b in enumerate(BLOCKS[gg][s]):
                    blocks(s, i, *b).start()

        @pl.when(g == gg)
        def _():
            for i, (k, a, e0, e1) in enumerate(OWN[gg]):
                pltpu.make_async_copy(hb_ref.at[k, e0:e1], hbuf.at[a, e0:e1], loc.at[2 + i]).start()

    start = {0: 2 - 2 * core, 1: w_far}
    half = {0: 2, 1: 1}
    keys = [(u, h, s) for u in (0,) for h in (0, 1) for s in (+1, -1)]
    s2 = {key + (p,): net.slot() for key in keys for p in (0, 1)}
    s2r = {key: net.slot() for key in keys}
    lead = {+1: 0, -1: 1}

    def place(h, dp):
        return lax.rem(mine[h] + 4 - dp, SIDE)

    def along(h, s):
        return dev(c, 1 - h, s)

    def second(h, s):
        return lax.rem(mine[1 - h] + 4 + s, SIDE)

    def rows(u, h, p, q):
        return yb.at[pl.ds(start[u] + p * half[u], half[u]), h, q]

    def send2(u, h):
        for first in (True, False):
            for s in (+1, -1):
                p = lead[s] if first else 1 - lead[s]
                ref = rows(u, h, p, mine[1 - h])
                net.copy(s2[u, h, s, p], ref, ref, along(h, s))

    def relay2(u, h):
        for s in (+1, -1):
            ref = rows(u, h, lead[s], second(h, -s))
            net.arrived(s2[u, h, s, lead[s]], ref, along(h, -s))
            net.copy(s2r[u, h, s], ref, ref, along(h, s))

    def last2(u, h):
        for s in (+1, -1):
            p = 1 - lead[s]
            net.arrived(s2[u, h, s, p], rows(u, h, p, second(h, -s)), along(h, -s))
            net.arrived(s2r[u, h, s], rows(u, h, lead[s], second(h, 2)), along(h, -s))

    def answer(when, answers):
        @pl.when(when)
        def _():
            pl.semaphore_wait(far_sem, answers)
            far_sends(0)

    answer((core == 0) & (c > 0), 1)
    for h in (0, 1):
        local[h].wait()
        for dp in OFFSETS:
            if dp:
                net.arrived(sl_own[h, dp], at(h, 2, 2, mine[1 - h], place(h, dp)), along(h, 1))
            net.arrived(sl_mate[h, dp], at(h, w_mate, 2, mine[1 - h], place(h, dp)), along(h, 1))
        send2(0, h)
    for h in (0, 1):
        relay2(0, h)
    for h in (0, 1):
        last2(0, h)
    answer(c == 0, SIDE * SIDE)

    def far_rows():
        for gg in (0, 1):
            for on in (0, 1):
                @pl.when((core == on) & (g == gg))
                def _():
                    k0, k1 = needed(on, gg)
                    net.arrived(got_far, yfar.at[k0:k1], (far, r))
        for k in (0, 1):
            yb[w_far + k, 0] = yfar[k, :, :, 0:8]
            for p in range(SIDE):
                for q in range(SIDE):
                    yb[w_far + k, 1, p, q] = yfar[k, q, p, 8:16]

    def far_band():
        for gg in (0, 1):
            @pl.when(g == gg)
            def _():
                for s in (+1, -1):
                    for i, b in enumerate(BLOCKS[gg][s]):
                        blocks(s, i, *b).wait_recv()
                for i, (k, a, e0, e1) in enumerate(OWN[gg]):
                    pltpu.make_async_copy(hb_ref.at[k, e0:e1], hbuf.at[a, e0:e1], loc.at[2 + i]).wait()
        between()

    def finish():
        for on in (0, 1):
            @pl.when(core == on)
            def _():
                for q in range(SIDE * SIDE):
                    far_copy(on, q).wait_send()
                far_blocks(on, lambda d: d.wait_send())
                for gg in (0, 1):
                    @pl.when(gd == gg)
                    def _():
                        s = 1 - 2 * on
                        for i, b in enumerate(BLOCKS[gg][s]):
                            blocks(s, i, *b).wait_send()
    return far_rows, far_band, finish


def cat3l(a, b):
    return jnp.concatenate([a, b, a], axis=1)


def vsum(e):
    return jnp.sum(e.reshape(-1, 8, e.shape[1]), axis=0)


def cdot(a, b):
    return dot(cat3l(*a), jnp.concatenate([b[0], b[0], b[1]], axis=0))


def fused(ncol, mask_hbm, fermi_hbm, hb_ref, mf_ref, out_ref, yb, hbuf, h_ref, yt_ref, x_ref, eh_ref, el_ref,
          stage, yfar, mask_ref, fermi_ref, send, recv, loc, near_sem, far_sem):
    c = lax.axis_index("cols")
    r = lax.axis_index("rep")
    y, x = lax.div(r, SIDE), lax.rem(r, SIDE)
    core = lax.rem(c, 2)
    g = lax.rem(y * (1 - core) + x * core, 2)
    gd = lax.rem(y * core + x * (1 - core), 2)
    other = r + (1 - 2 * g) * (4 - 3 * core)
    small = [pltpu.make_async_copy(mask_hbm, mask_ref, loc.at[4]), pltpu.make_async_copy(fermi_hbm, fermi_ref, loc.at[5])]
    for s in small:
        s.start()
    net = Net(send, recv)
    mask = []

    def between():
        for a in range(NC):
            for b in range(NC):
                sl = (slice(a * B, (a + 1) * B), slice(b * B, (b + 1) * B))
                if abs(a - b) <= 2:
                    w = 0.5 * mask[a] * mask[b]
                    h_ref[sl] = (hbuf[b, a - b + 2] + hbuf[a, b - a + 2].T) * w
                else:
                    h_ref[sl] = jnp.zeros((B, B), F32)

    far_rows, far_band, finish = gather(
        ncol, c, r, g, gd, hb_ref, mf_ref, yb, hbuf, net, loc, near_sem, far_sem, yfar, between)
    for o in small:
        o.wait()
    mask.extend(mask_ref[g, a].astype(F32) for a in range(NC))
    far_rows()
    mu = fermi_ref[0]
    ys = [yb[g + a].reshape(PS, B) * mask[a] for a in range(NC)]
    for a in range(NC):
        yt_ref[a * B:(a + 1) * B, :] = ys[a].T
    yt = split(yt_ref[...])
    yy = split(jnp.concatenate(ys, axis=1))
    eye = lax.broadcasted_iota(jnp.int32, (PS, PS), 0) == lax.broadcasted_iota(jnp.int32, (PS, PS), 1)
    k = cdot(yy, yt)
    ks = split(k)
    far_band()
    pt = cdot(split(h_ref[...]), yt)
    k2 = cdot(ks, ks)
    n = cdot(yy, split(pt))
    k3 = cdot(ks, split(k2))
    one = jnp.ones((1, 1), F32)
    sumsq = M * one + jnp.sum(vsum(jnp.where(eye, 2.0 * k, 0.0) + k * k), keepdims=True)
    cs = 2.0 * jnp.sqrt(sumsq / M)
    al = 1.0 / cs
    t = 0.5 * (3.0 - al)
    u = 0.5 * (3.0 - al * t * t)
    b0 = al * t * (t - al)
    b1 = al * al * (0.25 * al - t)
    b2 = 0.25 * al * al * al
    rs = lax.rsqrt(cs)
    q0 = (-0.5 * t * b0 - 0.5 * al * u) * rs
    q1 = (-0.5 * t * b1 + 0.25 * al * b0) * rs
    q2 = (-0.5 * t * b2 + 0.25 * al * b1) * rs
    q3 = (0.25 * al * b2) * rs
    a0 = t * u * rs
    rm = q1 * k + q2 * k2 + q3 * k3 + jnp.where(eye, q0, 0.0)
    rms = split(rm)
    rn = split(0.5 * cdot(rms, split(n)))
    both = cdot(yt, (jnp.concatenate([rms[0], rn[0]], axis=1), jnp.concatenate([rms[1], rn[1]], axis=1)))
    vts = split(both[:, :PS])
    pts = split(a0 * pt + both[:, PS:])
    a2 = a0 * a0
    lh, ll = (jnp.concatenate([pts[i], vts[i]], axis=1) for i in (0, 1))
    rh, rl = (jnp.concatenate([vts[i], pts[i]], axis=1) for i in (0, 1))
    lcat = cat3l(lh, ll)
    rcat = jnp.concatenate([rh, rh, rl], axis=1)

    def put(e, p, q):
        eh_ref[p:p + B, q:q + B], el_ref[p:p + B, q:q + B] = split(e)
        x_ref[p:p + B, q:q + B] = e

    total = jnp.zeros((8, B), F32)
    eye = lax.broadcasted_iota(jnp.int32, (B, B), 0) == lax.broadcasted_iota(jnp.int32, (B, B), 1)
    for c0, c1 in TILES:
        e = dot_nt(lcat[c0:], rcat[c0:c1]) + a2 * h_ref[c0:, c0:c1]
        for p in range(c0, M, B):
            for q in range(c0, c1, B):
                block = e[p - c0:p - c0 + B, q - c0:q - c0 + B]
                if p == q:
                    block = block - jnp.where(eye, mu, 0.0)
                if p >= c1:
                    total = total + 2.0 * vsum(block * block)
                    put(block.T, q, p)
                else:
                    total = total + vsum(block * block)
                put(block, p, q)
    acc = jnp.sum(total, keepdims=True)
    inv = 1.0 / (2.0 * jnp.sqrt(acc / M + 1e-5))

    def times(v, c0=0, c1=M):
        hi, lo = split(v)
        p = dot(jnp.concatenate([hi, lo], axis=0), eh_ref[:, c0:c1])
        return (p[:ROWS] + p[ROWS:] + dot(hi, el_ref[:, c0:c1])) * inv

    mine = pl.multiple_of(r * PIECE, 8)
    theirs = pl.multiple_of(other * PIECE, 8)
    x0 = jnp.concatenate([x_ref[pl.ds(mine, PIECE)], x_ref[pl.ds(theirs, PIECE)]], axis=0) * inv
    x1 = 1.5 * x0 - 0.5 * times(times(x0))
    p = times(x1)
    q = 1.5 * p - 0.5 * times(times(p))
    p = times(q)
    p2 = times(p)
    partner = (c, other)
    fs = [net.slot() for _ in TILES]
    for slot, (c0, c1) in zip(fs, TILES):
        x2 = 1.5 * x1[:, c0:c1] - 0.5 * (1.5 * p[:, c0:c1] - 0.5 * times(p2, c0, c1))
        ii = lax.broadcasted_iota(jnp.int32, (PIECE, c1 - c0), 0)
        jj = lax.broadcasted_iota(jnp.int32, (PIECE, c1 - c0), 1) + c0
        stage[:, c0:c1] = jnp.where(ii + theirs == jj, 0.5, 0.0) - 0.5 * x2[PIECE:]
        net.copy(slot, stage.at[:, c0:c1], out_ref.at[g, :, c0:c1], partner)
        out_ref[g, :, c0:c1] = jnp.where(ii + mine == jj, 0.5, 0.0) - 0.5 * x2[:PIECE]
    for s in net.sent:
        s.wait_send()
    finish()
    for slot, (c0, c1) in zip(fs, TILES):
        net.arrived(slot, out_ref.at[1 - g, :, c0:c1], partner)
    assert net.slots <= SLOTS


def on_device(ncol, hamiltonian_band, margin_factors, neighbour_mask, fermi_level):
    vm = pl.BlockSpec(memory_space=pltpu.VMEM)
    return pl.pallas_call(
        functools.partial(fused, ncol),
        out_shape=jax.ShapeDtypeStruct((2, PIECE, M), F32),
        in_specs=[pl.BlockSpec(memory_space=pltpu.HBM)] * 4,
        out_specs=vm,
        scratch_shapes=[
            pltpu.VMEM((6, 2, 4, 4, 8, B), F32),
            pltpu.VMEM((NC, NC, B, B), F32),
            pltpu.VMEM((M, M), F32),
            pltpu.VMEM((M, PS), F32),
            pltpu.VMEM((M, M), F32),
            pltpu.VMEM((M, M), BF),
            pltpu.VMEM((M, M), BF),
            pltpu.VMEM((PIECE, M), F32),
            pltpu.VMEM((2, SIDE, SIDE, 16, B), F32),
            pltpu.SMEM((2, NC), jnp.int32),
            pltpu.SMEM((1,), F32),
            pltpu.SemaphoreType.DMA((SLOTS,)),
            pltpu.SemaphoreType.DMA((SLOTS,)),
            pltpu.SemaphoreType.DMA((6,)),
            pltpu.SemaphoreType.REGULAR,
            pltpu.SemaphoreType.REGULAR,
        ],
        compiler_params=pltpu.CompilerParams(collective_id=0, has_side_effects=True, vmem_limit_bytes=(107 << 19)),
    )(neighbour_mask, fermi_level, hamiltonian_band, margin_factors)


def solution(mesh):
    in_specs = (P("cols", None, None, None), P("cols", "rep", None), P("cols", None), P())
    return jax.shard_map(
        functools.partial(on_device, mesh.shape["cols"]), mesh=mesh, in_specs=in_specs,
        out_specs=P("cols", "rep", None), check_vma=False)
```

```python
import functools
import jax, jax.numpy as jnp
from jax import lax
from jax.experimental import pallas as pl
from jax.experimental.pallas import tpu as pltpu
from jax.sharding import PartitionSpec as P

B = 128
NC = 5
M = 640
PS = 256
ROWS = 80
PIECE = 40
SIDE = 4
F32 = jnp.float32
BF = jnp.bfloat16
MESH = pl.DeviceIdType.MESH


def split(x):
    hi = x.astype(BF)
    return hi, (x - hi.astype(F32)).astype(BF)


def dot(a, b):
    return jnp.dot(a, b, preferred_element_type=F32)


def dot_nt(a, b):
    return lax.dot_general(a, b, (((1,), (1,)), ((), ())), preferred_element_type=F32)


def dot3(a, b, d=dot):
    (ah, al), (bh, bl) = a, b
    return d(ah, bh) + d(ah, bl) + d(al, bh)


class Net:
    def __init__(self, send, recv):
        self.send, self.recv = send, recv
        self.slots = 0
        self.sent = []

    def slot(self):
        self.slots += 1
        return self.slots - 1

    def copy(self, slot, src, dst, dev):
        c = pltpu.make_async_remote_copy(
            src_ref=src, dst_ref=dst, send_sem=self.send.at[slot], recv_sem=self.recv.at[slot],
            device_id=dev, device_id_type=MESH)
        c.start()
        self.sent.append(c)

    def arrived(self, slot, dst, dev):
        pltpu.make_async_remote_copy(
            src_ref=dst, dst_ref=dst, send_sem=self.send.at[slot], recv_sem=self.recv.at[slot],
            device_id=dev, device_id_type=MESH).wait_recv()


SLOTS = 64
TILES = ((0, 256), (256, 512), (512, 640))
BLOCKS = {
    0: {+1: ((1, 1, 1, 5), (0, 0, 2, 3), (0, 0, 3, 5)), -1: ((0, 4, 0, 3),)},
    1: {+1: ((1, 0, 2, 5),), -1: ((0, 3, 0, 4), (1, 4, 2, 3), (1, 4, 0, 2))},
}
OWN = {0: ((0, 2, 0, 5), (1, 3, 0, 4)), 1: ((1, 2, 0, 5), (0, 1, 1, 5))}
OFFSETS = (0, 1, 3, 2)


def gather(ncol, c, r, g, gd, hb_ref, mf_ref, yb, hbuf, net, loc, near_sem, far_sem, yfar, between):
    y, x = lax.div(r, SIDE), lax.rem(r, SIDE)
    core = lax.rem(c, 2)
    mate = c + 1 - 2 * core
    far = lax.rem(c + ncol - 1 + 2 * core, ncol)

    def dev(col, h, dp):
        if h == 0:
            return (col, y * SIDE + (lax.rem(x + dp + 4, SIDE) if dp else x))
        return (col, (lax.rem(y + dp + 4, SIDE) if dp else y) * SIDE + x)

    def cross(col):
        return [dev(col, h, dp) for h in (0, 1) for dp in OFFSETS if not (dp == 0 and h == 1)]

    def greet(sem, d):
        pl.semaphore_signal(sem, inc=1, device_id=d, device_id_type=MESH)

    barrier = pltpu.get_barrier_semaphore()
    home = c - core

    @pl.when(core == 0)
    def _():
        for d in cross(c)[1:]:
            greet(barrier, d)
        for q in range(SIDE * SIDE):
            greet(barrier, (far, q))

    @pl.when(core == 1)
    def _():
        for d in cross(home):
            greet(barrier, d)

    inner = core * (1 - lax.div(c + 1, ncol))

    @pl.when(inner == 1)
    def _():
        for q in range(1, SIDE * SIDE):
            greet(barrier, (c, lax.rem(r + q, SIDE * SIDE)))
    pl.semaphore_wait(barrier, 13 + 3 * core + 15 * inner)

    mine = {0: x, 1: y}

    def at(h, w, n, second, first):
        return yb.at[pl.ds(w, n), h, second, first]

    def own(h):
        return mf_ref.at[:, 8 * h:8 * h + 8]

    w_mate, w_far = 4 * (1 - core), 4 * core
    sl_own = {(h, dp): net.slot() for h in (0, 1) for dp in OFFSETS[1:]}
    sl_mate = {(h, dp): net.slot() for h in (0, 1) for dp in OFFSETS}
    sl_far = [net.slot() for _ in range(SIDE * SIDE)]
    got_far = sl_far[0]
    hs = {(s, i): net.slot() for s in (+1, -1) for i in (0, 1, 2)}

    def needed(to_core, gg):
        return ((0, 2) if gg == 0 else (1, 2)) if to_core == 0 else ((0, 1) if gg == 0 else (0, 2))

    def far_copy(on, q):
        k0, k1 = needed(1 - on, q // SIDE % 2 if on else q % 2)
        return pltpu.make_async_remote_copy(
            src_ref=mf_ref.at[k0:k1], dst_ref=yfar.at[k0:k1, y, x],
            send_sem=net.send.at[sl_far[q]], recv_sem=net.recv.at[got_far],
            device_id=(far, q), device_id_type=MESH)

    def blocks(s, i, k, a, e0, e1, shift=0):
        to = lax.rem(c + ncol + s, ncol)
        return pltpu.make_async_remote_copy(
            src_ref=hb_ref.at[k, e0:e1], dst_ref=hbuf.at[a, e0:e1], send_sem=net.send.at[hs[s, i]],
            recv_sem=net.recv.at[hs[s, i]], device_id=(to, r - shift), device_id_type=MESH)

    def far_blocks(on, op):
        for gg in (0, 1):
            @pl.when(gd == gg)
            def _():
                s = 2 * on - 1
                for i, b in enumerate(BLOCKS[gg][s]):
                    if i < 2:
                        op(blocks(s, i, *b))
                if (on, gg) == (1, 1):
                    op(blocks(+1, 2, *BLOCKS[0][+1][2], shift=SIDE))
                if (on, gg) == (0, 0):
                    op(blocks(-1, 2, *BLOCKS[1][-1][2], shift=-1))

    def far_sends(on):
        for q in range(SIDE * SIDE):
            far_copy(on, q).start()
        far_blocks(on, lambda d: d.start())

    @pl.when(core == 0)
    def _():
        greet(near_sem, (mate, r))

    @pl.when(core == 1)
    def _():
        greet(far_sem, (far, r))

        @pl.when(inner == 0)
        def _():
            for q in range(1, SIDE * SIDE):
                greet(far_sem, (far, lax.rem(r + q, SIDE * SIDE)))
        far_sends(1)
        pl.semaphore_wait(near_sem, 1)
    for dp in (2, 1, 3, 0):
        for h in (0, 1):
            net.copy(sl_mate[h, dp], own(h), at(h, 4 * core, 2, mine[1 - h], mine[h]), dev(mate, h, dp))
            if dp:
                net.copy(sl_own[h, dp], own(h), at(h, 2, 2, mine[1 - h], mine[h]), dev(c, h, dp))
    local = []
    for h in (0, 1):
        l = pltpu.make_async_copy(own(h), at(h, 2, 2, mine[1 - h], mine[h]), loc.at[h])
        l.start()
        local.append(l)
    for gg in (0, 1):
        for on in (0, 1):
            @pl.when((core == on) & (gd == gg))
            def _():
                s = 1 - 2 * on
                for i, b in enumerate(BLOCKS[gg][s]):
                    blocks(s, i, *b).start()

        @pl.when(g == gg)
        def _():
            for i, (k, a, e0, e1) in enumerate(OWN[gg]):
                pltpu.make_async_copy(hb_ref.at[k, e0:e1], hbuf.at[a, e0:e1], loc.at[2 + i]).start()

    start = {0: 2 - 2 * core, 1: w_far}
    half = {0: 2, 1: 1}
    keys = [(u, h, s) for u in (0,) for h in (0, 1) for s in (+1, -1)]
    s2 = {key + (p,): net.slot() for key in keys for p in (0, 1)}
    s2r = {key: net.slot() for key in keys}
    lead = {+1: 0, -1: 1}

    def place(h, dp):
        return lax.rem(mine[h] + 4 - dp, SIDE)

    def along(h, s):
        return dev(c, 1 - h, s)

    def second(h, s):
        return lax.rem(mine[1 - h] + 4 + s, SIDE)

    def rows(u, h, p, q):
        return yb.at[pl.ds(start[u] + p * half[u], half[u]), h, q]

    def send2(u, h):
        for first in (True, False):
            for s in (+1, -1):
                p = lead[s] if first else 1 - lead[s]
                ref = rows(u, h, p, mine[1 - h])
                net.copy(s2[u, h, s, p], ref, ref, along(h, s))

    def relay2(u, h):
        for s in (+1, -1):
            ref = rows(u, h, lead[s], second(h, -s))
            net.arrived(s2[u, h, s, lead[s]], ref, along(h, -s))
            net.copy(s2r[u, h, s], ref, ref, along(h, s))

    def last2(u, h):
        for s in (+1, -1):
            p = 1 - lead[s]
            net.arrived(s2[u, h, s, p], rows(u, h, p, second(h, -s)), along(h, -s))
            net.arrived(s2r[u, h, s], rows(u, h, lead[s], second(h, 2)), along(h, -s))

    def answer(when, answers):
        @pl.when(when)
        def _():
            pl.semaphore_wait(far_sem, answers)
            far_sends(0)

    for h in (0, 1):
        local[h].wait()
        for dp in OFFSETS:
            if dp:
                net.arrived(sl_own[h, dp], at(h, 2, 2, mine[1 - h], place(h, dp)), along(h, 1))
            net.arrived(sl_mate[h, dp], at(h, w_mate, 2, mine[1 - h], place(h, dp)), along(h, 1))
        send2(0, h)
        if h == 0:
            answer((core == 0) & (c > 0), 1)
    for h in (0, 1):
        relay2(0, h)
    for h in (0, 1):
        last2(0, h)
    answer(c == 0, SIDE * SIDE)

    def far_rows():
        for gg in (0, 1):
            for on in (0, 1):
                @pl.when((core == on) & (g == gg))
                def _():
                    k0, k1 = needed(on, gg)
                    net.arrived(got_far, yfar.at[k0:k1], (far, r))
        for k in (0, 1):
            yb[w_far + k, 0] = yfar[k, :, :, 0:8]
            for p in range(SIDE):
                for q in range(SIDE):
                    yb[w_far + k, 1, p, q] = yfar[k, q, p, 8:16]

    def far_band():
        for gg in (0, 1):
            @pl.when(g == gg)
            def _():
                for s in (+1, -1):
                    for i, b in enumerate(BLOCKS[gg][s]):
                        blocks(s, i, *b).wait_recv()
                for i, (k, a, e0, e1) in enumerate(OWN[gg]):
                    pltpu.make_async_copy(hb_ref.at[k, e0:e1], hbuf.at[a, e0:e1], loc.at[2 + i]).wait()
        between()

    def finish():
        for on in (0, 1):
            @pl.when(core == on)
            def _():
                for q in range(SIDE * SIDE):
                    far_copy(on, q).wait_send()
                far_blocks(on, lambda d: d.wait_send())
                for gg in (0, 1):
                    @pl.when(gd == gg)
                    def _():
                        s = 1 - 2 * on
                        for i, b in enumerate(BLOCKS[gg][s]):
                            blocks(s, i, *b).wait_send()
    return far_rows, far_band, finish


def cat3l(a, b):
    return jnp.concatenate([a, b, a], axis=1)


def vsum(e):
    return jnp.sum(e.reshape(-1, 8, e.shape[1]), axis=0)


def cdot(a, b):
    return dot(cat3l(*a), jnp.concatenate([b[0], b[0], b[1]], axis=0))


def fused(ncol, mask_hbm, fermi_hbm, hb_ref, mf_ref, out_ref, yb, hbuf, h_ref, yt_ref, x_ref, eh_ref, el_ref,
          stage, yfar, mask_ref, fermi_ref, send, recv, loc, near_sem, far_sem):
    c = lax.axis_index("cols")
    r = lax.axis_index("rep")
    y, x = lax.div(r, SIDE), lax.rem(r, SIDE)
    core = lax.rem(c, 2)
    g = lax.rem(y * (1 - core) + x * core, 2)
    gd = lax.rem(y * core + x * (1 - core), 2)
    other = r + (1 - 2 * g) * (4 - 3 * core)
    small = [pltpu.make_async_copy(mask_hbm, mask_ref, loc.at[4]), pltpu.make_async_copy(fermi_hbm, fermi_ref, loc.at[5])]
    for s in small:
        s.start()
    net = Net(send, recv)
    mask = []

    def between():
        for a in range(NC):
            for b in range(NC):
                sl = (slice(a * B, (a + 1) * B), slice(b * B, (b + 1) * B))
                if abs(a - b) <= 2:
                    w = 0.5 * mask[a] * mask[b]
                    h_ref[sl] = (hbuf[b, a - b + 2] + hbuf[a, b - a + 2].T) * w
                else:
                    h_ref[sl] = jnp.zeros((B, B), F32)

    far_rows, far_band, finish = gather(
        ncol, c, r, g, gd, hb_ref, mf_ref, yb, hbuf, net, loc, near_sem, far_sem, yfar, between)
    for o in small:
        o.wait()
    mask.extend(mask_ref[g, a].astype(F32) for a in range(NC))
    far_rows()
    mu = fermi_ref[0]
    ys = [yb[g + a].reshape(PS, B) * mask[a] for a in range(NC)]
    for a in range(NC):
        yt_ref[a * B:(a + 1) * B, :] = ys[a].T
    yt = split(yt_ref[...])
    yy = split(jnp.concatenate(ys, axis=1))
    eye = lax.broadcasted_iota(jnp.int32, (PS, PS), 0) == lax.broadcasted_iota(jnp.int32, (PS, PS), 1)
    k = cdot(yy, yt)
    ks = split(k)
    far_band()
    pt = cdot(split(h_ref[...]), yt)
    k2 = cdot(ks, ks)
    n = cdot(yy, split(pt))
    k3 = cdot(ks, split(k2))
    one = jnp.ones((1, 1), F32)
    sumsq = M * one + jnp.sum(vsum(jnp.where(eye, 2.0 * k, 0.0) + k * k), keepdims=True)
    cs = 2.0 * jnp.sqrt(sumsq / M)
    al = 1.0 / cs
    t = 0.5 * (3.0 - al)
    u = 0.5 * (3.0 - al * t * t)
    b0 = al * t * (t - al)
    b1 = al * al * (0.25 * al - t)
    b2 = 0.25 * al * al * al
    rs = lax.rsqrt(cs)
    q0 = (-0.5 * t * b0 - 0.5 * al * u) * rs
    q1 = (-0.5 * t * b1 + 0.25 * al * b0) * rs
    q2 = (-0.5 * t * b2 + 0.25 * al * b1) * rs
    q3 = (0.25 * al * b2) * rs
    a0 = t * u * rs
    rm = q1 * k + q2 * k2 + q3 * k3 + jnp.where(eye, q0, 0.0)
    rms = split(rm)
    rn = split(0.5 * cdot(rms, split(n)))
    both = cdot(yt, (jnp.concatenate([rms[0], rn[0]], axis=1), jnp.concatenate([rms[1], rn[1]], axis=1)))
    vts = split(both[:, :PS])
    pts = split(a0 * pt + both[:, PS:])
    a2 = a0 * a0
    lh, ll = (jnp.concatenate([pts[i], vts[i]], axis=1) for i in (0, 1))
    rh, rl = (jnp.concatenate([vts[i], pts[i]], axis=1) for i in (0, 1))
    lcat = cat3l(lh, ll)
    rcat = jnp.concatenate([rh, rh, rl], axis=1)

    def put(e, p, q):
        eh_ref[p:p + B, q:q + B], el_ref[p:p + B, q:q + B] = split(e)
        x_ref[p:p + B, q:q + B] = e

    total = jnp.zeros((8, B), F32)
    eye = lax.broadcasted_iota(jnp.int32, (B, B), 0) == lax.broadcasted_iota(jnp.int32, (B, B), 1)
    for c0, c1 in TILES:
        e = dot_nt(lcat[c0:], rcat[c0:c1]) + a2 * h_ref[c0:, c0:c1]
        for p in range(c0, M, B):
            for q in range(c0, c1, B):
                block = e[p - c0:p - c0 + B, q - c0:q - c0 + B]
                if p == q:
                    block = block - jnp.where(eye, mu, 0.0)
                if p >= c1:
                    total = total + 2.0 * vsum(block * block)
                    put(block.T, q, p)
                else:
                    total = total + vsum(block * block)
                put(block, p, q)
    acc = jnp.sum(total, keepdims=True)
    inv = 1.0 / (2.0 * jnp.sqrt(acc / M + 1e-5))

    def times(v, c0=0, c1=M):
        hi, lo = split(v)
        p = dot(jnp.concatenate([hi, lo], axis=0), eh_ref[:, c0:c1])
        return (p[:ROWS] + p[ROWS:] + dot(hi, el_ref[:, c0:c1])) * inv

    mine = pl.multiple_of(r * PIECE, 8)
    theirs = pl.multiple_of(other * PIECE, 8)
    x0 = jnp.concatenate([x_ref[pl.ds(mine, PIECE)], x_ref[pl.ds(theirs, PIECE)]], axis=0) * inv
    x1 = 1.5 * x0 - 0.5 * times(times(x0))
    p = times(x1)
    q = 1.5 * p - 0.5 * times(times(p))
    p = times(q)
    p2 = times(p)
    partner = (c, other)
    fs = [net.slot() for _ in TILES]
    for slot, (c0, c1) in zip(fs, TILES):
        x2 = 1.5 * x1[:, c0:c1] - 0.5 * (1.5 * p[:, c0:c1] - 0.5 * times(p2, c0, c1))
        ii = lax.broadcasted_iota(jnp.int32, (PIECE, c1 - c0), 0)
        jj = lax.broadcasted_iota(jnp.int32, (PIECE, c1 - c0), 1) + c0
        stage[:, c0:c1] = jnp.where(ii + theirs == jj, 0.5, 0.0) - 0.5 * x2[PIECE:]
        net.copy(slot, stage.at[:, c0:c1], out_ref.at[g, :, c0:c1], partner)
        out_ref[g, :, c0:c1] = jnp.where(ii + mine == jj, 0.5, 0.0) - 0.5 * x2[:PIECE]
    for s in net.sent:
        s.wait_send()
    finish()
    for slot, (c0, c1) in zip(fs, TILES):
        net.arrived(slot, out_ref.at[1 - g, :, c0:c1], partner)
    assert net.slots <= SLOTS


def on_device(ncol, hamiltonian_band, margin_factors, neighbour_mask, fermi_level):
    vm = pl.BlockSpec(memory_space=pltpu.VMEM)
    return pl.pallas_call(
        functools.partial(fused, ncol),
        out_shape=jax.ShapeDtypeStruct((2, PIECE, M), F32),
        in_specs=[pl.BlockSpec(memory_space=pltpu.HBM)] * 4,
        out_specs=vm,
        scratch_shapes=[
            pltpu.VMEM((6, 2, 4, 4, 8, B), F32),
            pltpu.VMEM((NC, NC, B, B), F32),
            pltpu.VMEM((M, M), F32),
            pltpu.VMEM((M, PS), F32),
            pltpu.VMEM((M, M), F32),
            pltpu.VMEM((M, M), BF),
            pltpu.VMEM((M, M), BF),
            pltpu.VMEM((PIECE, M), F32),
            pltpu.VMEM((2, SIDE, SIDE, 16, B), F32),
            pltpu.SMEM((2, NC), jnp.int32),
            pltpu.SMEM((1,), F32),
            pltpu.SemaphoreType.DMA((SLOTS,)),
            pltpu.SemaphoreType.DMA((SLOTS,)),
            pltpu.SemaphoreType.DMA((6,)),
            pltpu.SemaphoreType.REGULAR,
            pltpu.SemaphoreType.REGULAR,
        ],
        compiler_params=pltpu.CompilerParams(collective_id=0, has_side_effects=True, vmem_limit_bytes=(107 << 19)),
    )(neighbour_mask, fermi_level, hamiltonian_band, margin_factors)


def solution(mesh):
    in_specs = (P("cols", None, None, None), P("cols", "rep", None), P("cols", None), P())
    return jax.shard_map(
        functools.partial(on_device, mesh.shape["cols"]), mesh=mesh, in_specs=in_specs,
        out_specs=P("cols", "rep", None), check_vma=False)
```
